128 devices in a mesh: row: 8 (over x, core), col: 16 (over y, z).
Axes of the slice: x: 4, y: 4, z: 4, core: 2. Of those that a mesh axis runs over, the one named last changes fastest.
Arguments:
- features: bfloat16 [65536, 1024], P(('row', 'col')), may hold values from -6 to 6
- neighbours: int32 [65536, 16], P(('row', 'col')), may hold values from 0 to 3583, as said below
- degrees: int32 [65536], P(('row', 'col')), may hold values from 1 to 16, as said below
- send_rows: int32 [128, 2048], P(('row', 'col')), may hold values from 0 to 511
- send_count: int32 [128, 128], P(('row', 'col')), may hold values from 8 to 16, as said below
- hub_rows: int32 [1024], P(('row', 'col')), may hold values from 0 to 511, as said below
- w_self: bfloat16 [1024, 1024], replicated, may hold values from -0.1875 to 0.1875
- w_neigh: bfloat16 [1024, 1024], replicated, may hold values from -0.1875 to 0.1875
- bias_term: float32 [1024], replicated, may hold values from -3 to 3
- cotangent: bfloat16 [65536, 1024], P(('row', 'col')), may hold values from -6 to 6
Outputs:
- hidden: bfloat16 [65536, 1024], P(('row', 'col'))
- grad_x: bfloat16 [65536, 1024], P(('row', 'col'))
- grad_self: bfloat16 [1024, 1024], replicated
- grad_neigh: bfloat16 [1024, 1024], replicated
The draws below stay inside these ranges and needn't reach their ends.
Inputs may be any that keep to these rules, and one draw needn't show every extreme that they name: neighbours of partition d point to its own rows (below 512), to live slots of arrived_d only (row 512 + p * 16 + s with p != d and s < send_count[p, d]), or to hub rows; entries at j >= degrees[i] also lie in the table. `degrees`: every seed has at least one neighbour. `send_count`: each partition sends between 8 and 16 live rows to each partition, and exactly 16 to the next one. `hub_rows`: the 8 hub rows of a partition are distinct.
All inputs are finite; a program needn't handle non-finite values.
Results may differ from the reference program's by a relative error of at most 0.0064.
Values may be sent and summed in bfloat16 or wider, within the bound.
A program may use at most 128 MiB of HBM per device.

```python
import jax
import jax.numpy as jnp
from jax import lax

D = 1024
NODE_DEV = 512
FANOUT = 16
CAP = 16
HUB_DEV = 8
PEERS = 128
NODES = 65536
HUBS = 1024
SLOTS = 2048
N_ROW = 8
N_COL = 16


def count_table(key):
    n_dev = NODES // NODE_DEV
    base_key = jax.random.fold_in(key, 11)
    low_count = CAP // 2
    counts = low_count + jax.random.randint(base_key, (n_dev, n_dev), 0, CAP - low_count + 1)
    dev_ids = jnp.arange(n_dev, dtype=jnp.int32)
    next_one = (dev_ids[:, None] + 1) % n_dev == dev_ids[None, :]
    return jnp.where(next_one, CAP, counts).astype(jnp.int32)


def draw_send_count(key, part):
    return count_table(key)


def draw_neighbours(key, part):
    n_dev = NODES // NODE_DEV
    counts = count_table(key)
    base_key = jax.random.fold_in(key, 23)
    sub_keys = jax.random.split(base_key, 6)
    shape = (NODES, FANOUT)
    owner_dev = (jnp.arange(NODES, dtype=jnp.int32) // NODE_DEV)[:, None] * jnp.ones(shape, jnp.int32)
    pick_kind = jax.random.randint(sub_keys[0], shape, 0, 8)
    local_ids = jax.random.randint(sub_keys[1], shape, 0, NODE_DEV)
    offset = jax.random.randint(sub_keys[2], shape, 1, n_dev)
    peer_dev = (owner_dev + offset) % n_dev
    slot_limit = counts[peer_dev, owner_dev]
    slot_ids = jax.random.randint(sub_keys[3], shape, 0, slot_limit)
    remote_ids = NODE_DEV + peer_dev * CAP + slot_ids
    hub_first = jax.random.randint(sub_keys[4], shape, 0, HUBS)
    hub_second = jax.random.randint(sub_keys[5], shape, 0, HUBS)
    hub_ids = NODE_DEV + n_dev * CAP + hub_first * hub_second // HUBS
    chosen = jnp.where(pick_kind < 4, local_ids, jnp.where(pick_kind < 6, remote_ids, hub_ids))
    chosen = chosen.at[0, 0].set(NODE_DEV + n_dev * CAP + HUBS - 1)
    chosen = chosen.at[0, 1].set(0)
    return chosen.astype(jnp.int32)


def draw_degrees(key, part):
    base_key = jax.random.fold_in(key, 37)
    drawn = jax.random.randint(base_key, (NODES,), 1, FANOUT + 1)
    return drawn.at[0].set(FANOUT).astype(jnp.int32)


def draw_hub_rows(key, part):
    n_dev = NODES // NODE_DEV
    base_key = jax.random.fold_in(key, 41)
    perm_key, shift_key = jax.random.split(base_key)
    sub_keys = jax.random.split(perm_key, n_dev)
    shifts = jax.random.randint(shift_key, (n_dev,), 0, NODE_DEV)
    shifts = shifts.at[0].set(0).at[1].set(NODE_DEV - 1)

    def one_part(one_key, shift):
        perm = jax.random.permutation(one_key, NODE_DEV)
        return ((perm - perm[0] + shift) % NODE_DEV)[:HUB_DEV]
    chosen = jax.vmap(one_part)(sub_keys, shifts)
    return chosen.reshape(-1).astype(jnp.int32)


def plant(entries, rng, least, top_value):
    dims = entries.shape
    place = [jax.random.randint(jax.random.fold_in(rng, axis), (), 0, dims[axis]) for axis in range(len(dims))]
    entries = entries.at[tuple(place)].set(least)
    longest = dims.index(max(dims))
    place[longest] = (place[longest] + 1) % dims[longest]
    return entries.at[tuple(place)].set(top_value)


def levels(stream_key, dims, shards, low, high):
    def one(axis_at, shards_of):
        steps = jax.random.uniform(jax.random.fold_in(jax.random.fold_in(stream_key, 6), axis_at), (shards_of,), jnp.float32, low / len(shards), high / len(shards))
        return jnp.repeat(jnp.exp(steps), dims[axis_at] // shards_of).reshape((-1,) + (1,) * (len(dims) - axis_at - 1))

    level = one(*shards[0])
    for cut in shards[1:]:
        level = level * one(*cut)
    return level


def bell_draw(stream_key, dims, spread, reach, shards=(), kind=jnp.bfloat16):
    values = jax.random.normal(stream_key, dims, jnp.float32) * spread
    if len(shards) > 0:
        values = levels(stream_key, dims, shards, -0.22, 0.18) * values
    return jnp.clip(values, min=-reach, max=reach).astype(kind)


def setup_inputs(seed: int = 0) -> dict:
    streams_of = jax.random.split(jax.random.key(seed), 11)
    features = bell_draw(streams_of[0], (NODES, D), 1.0, 6.0, ((0, 128),))
    neighbours = draw_neighbours(jax.random.fold_in(streams_of[10], 71), 0)
    degrees = draw_degrees(jax.random.fold_in(streams_of[10], 71), 0)
    send_rows = plant(jax.random.randint(streams_of[3], (PEERS, SLOTS), 0, NODE_DEV), jax.random.fold_in(streams_of[3], 1), 0, NODE_DEV - 1).astype(jnp.int32)
    send_count = draw_send_count(jax.random.fold_in(streams_of[10], 71), 0)
    hub_rows = draw_hub_rows(jax.random.fold_in(streams_of[10], 71), 0)
    w_self = bell_draw(streams_of[6], (D, D), D ** -0.5, 0.1875)
    w_neigh = bell_draw(streams_of[7], (D, D), D ** -0.5, 0.1875)
    bias_term = bell_draw(streams_of[8], (D,), 0.5, 3.0, (), jnp.float32)
    cotangent = bell_draw(streams_of[9], (NODES, D), 1.0, 6.0, ((0, 128),))
    return {"features": features, "neighbours": neighbours, "degrees": degrees, "send_rows": send_rows, "send_count": send_count, "hub_rows": hub_rows, "w_self": w_self, "w_neigh": w_neigh, "bias_term": bias_term, "cotangent": cotangent}


def silu_slope(pre_act):
    sigmoid_val = jax.nn.sigmoid(pre_act)
    return sigmoid_val * (1.0 + pre_act * (1.0 - sigmoid_val))


def reference(features, neighbours, degrees, send_rows, send_count, hub_rows, w_self, w_neigh, bias_term, cotangent):
    n_dev = N_ROW * N_COL
    feat_width = features.shape[1]
    tile_size = min(512, NODE_DEV)
    n_tiles = NODE_DEV // tile_size
    hub_owner = jnp.arange(n_dev * HUB_DEV, dtype=jnp.int32) // HUB_DEV
    hub_global = (hub_owner * NODE_DEV + hub_rows).astype(jnp.int32)
    all_hubs = features[hub_global]
    slot_index = jnp.arange(CAP, dtype=jnp.int32)
    source_ids = jnp.arange(n_dev, dtype=jnp.int32)
    table_len = NODE_DEV + n_dev * CAP + n_dev * HUB_DEV
    fan_index = jnp.arange(FANOUT, dtype=jnp.int32)

    def per_device(state_carry, device):
        grad_acc, self_acc, neigh_acc = state_carry
        base = (device * NODE_DEV).astype(jnp.int32)
        own_rows = lax.dynamic_slice_in_dim(features, base, NODE_DEV, 0)
        own_cot = lax.dynamic_slice_in_dim(cotangent, base, NODE_DEV, 0)
        own_nbrs = lax.dynamic_slice_in_dim(neighbours, base, NODE_DEV, 0)
        own_degs = lax.dynamic_slice_in_dim(degrees, base, NODE_DEV, 0)
        incoming_rows = lax.dynamic_slice_in_dim(send_rows, (device * CAP).astype(jnp.int32), CAP, 1)
        incoming_live = slot_index[None, :] < send_count[:, device][:, None]
        incoming_global = (source_ids[:, None] * NODE_DEV + incoming_rows).astype(jnp.int32)
        arrived = jnp.where(incoming_live[:, :, None], features[incoming_global], jnp.zeros((), features.dtype))
        arrived = arrived.reshape(n_dev * CAP, feat_width)
        src_table = jnp.concatenate([own_rows, arrived, all_hubs], 0)
        live_mask = fan_index[None, :] < own_degs[:, None]
        inv_deg = 1.0 / own_degs.astype(jnp.float32)

        def gather_tile(tile_index):
            tile_start = (tile_index * tile_size).astype(jnp.int32)
            tile_nbrs = lax.dynamic_slice_in_dim(own_nbrs, tile_start, tile_size, 0)
            tile_live = lax.dynamic_slice_in_dim(live_mask, tile_start, tile_size, 0)
            picked = src_table[tile_nbrs].astype(jnp.float32)
            return jnp.sum(jnp.where(tile_live[:, :, None], picked, 0.0), axis=1)

        summed = lax.map(gather_tile, jnp.arange(n_tiles, dtype=jnp.int32)).reshape(NODE_DEV, feat_width)
        aggregate = (summed * inv_deg[:, None]).astype(jnp.bfloat16)
        pre_act = (jnp.dot(own_rows, w_self, preferred_element_type=jnp.float32)
                   + jnp.dot(aggregate, w_neigh, preferred_element_type=jnp.float32)
                   + bias_term.astype(jnp.float32)[None, :])
        hidden = jax.nn.silu(pre_act).astype(jnp.bfloat16)
        d_pre = (own_cot.astype(jnp.float32) * silu_slope(pre_act)).astype(jnp.bfloat16)
        self_acc = self_acc + lax.dot_general(own_rows, d_pre, (((0,), (0,)), ((), ())), preferred_element_type=jnp.float32)
        neigh_acc = neigh_acc + lax.dot_general(aggregate, d_pre, (((0,), (0,)), ((), ())), preferred_element_type=jnp.float32)
        d_agg = lax.dot_general(d_pre, w_neigh, (((1,), (1,)), ((), ())), preferred_element_type=jnp.float32) * inv_deg[:, None]
        d_own = lax.dot_general(d_pre, w_self, (((1,), (1,)), ((), ())), preferred_element_type=jnp.float32)

        def spread_tile(tile_index, d_table):
            tile_start = (tile_index * tile_size).astype(jnp.int32)
            tile_nbrs = lax.dynamic_slice_in_dim(own_nbrs, tile_start, tile_size, 0)
            tile_live = lax.dynamic_slice_in_dim(live_mask, tile_start, tile_size, 0)
            tile_grad = lax.dynamic_slice_in_dim(d_agg, tile_start, tile_size, 0)
            target = jnp.where(tile_live, tile_nbrs, table_len).astype(jnp.int32)
            updates = jnp.broadcast_to(tile_grad[:, None, :], (tile_size, FANOUT, feat_width))
            return d_table.at[target.reshape(-1)].add(updates.reshape(-1, feat_width), mode="drop")

        d_table = lax.fori_loop(0, n_tiles, spread_tile, jnp.zeros((table_len, feat_width), jnp.float32))
        d_local = d_table[:NODE_DEV]
        d_arrived = d_table[NODE_DEV:NODE_DEV + n_dev * CAP]
        d_hubs = d_table[NODE_DEV + n_dev * CAP:]
        own_ids = (base + jnp.arange(NODE_DEV, dtype=jnp.int32)).astype(jnp.int32)
        grad_acc = grad_acc.at[own_ids].add(d_own + d_local)
        d_arrived = jnp.where(incoming_live.reshape(-1, 1), d_arrived, 0.0)
        grad_acc = grad_acc.at[incoming_global.reshape(-1)].add(d_arrived)
        grad_acc = grad_acc.at[hub_global].add(d_hubs)
        return (grad_acc, self_acc, neigh_acc), hidden

    init_state = (jnp.zeros((n_dev * NODE_DEV, feat_width), jnp.float32),
                  jnp.zeros((feat_width, feat_width), jnp.float32),
                  jnp.zeros((feat_width, feat_width), jnp.float32))
    final_state, hidden_all = lax.scan(per_device, init_state, jnp.arange(n_dev, dtype=jnp.int32))
    grad_acc, self_acc, neigh_acc = final_state
    return (hidden_all.reshape(n_dev * NODE_DEV, feat_width), grad_acc.astype(jnp.bfloat16),
            self_acc.astype(jnp.bfloat16), neigh_acc.astype(jnp.bfloat16))
```

```python
import functools
import jax
import jax.numpy as jnp
from jax import lax
from jax.experimental import pallas as pl
from jax.experimental.pallas import tpu as pltpu
from jax.sharding import PartitionSpec as P

MESH = pl.DeviceIdType.MESH
COLS = ((0, 384), (384, 384), (768, 256))
ORDERS = (("x", "y", "z"), ("y", "z", "x"), ("z", "x", "y"))


def where_am_i():
    row = lax.axis_index("row")
    col = lax.axis_index("col")
    return {"x": row // 2, "core": lax.rem(row, 2), "y": col // 4, "z": lax.rem(col, 4)}


def device_at(place):
    return (place["x"] * 2 + place["core"], place["y"] * 4 + place["z"])


def shifted(place, dim, step):
    other = dict(place)
    other[dim] = lax.rem(place[dim] + step, 2 if dim == "core" else 4)
    return other


def greet(place):
    barrier = pltpu.get_barrier_semaphore()
    peers = [shifted(place, "core", 1)]
    peers += [shifted(place, dim, step) for dim in "xyz" for step in (1, 2, 3)]
    for peer in peers:
        pl.semaphore_signal(barrier, inc=1, device_id=device_at(peer), device_id_type=MESH)
    pl.semaphore_wait(barrier, len(peers))


def remote(src, dst, send_sem, recv_sem, peer):
    return pltpu.make_async_remote_copy(
        src_ref=src,
        dst_ref=dst,
        send_sem=send_sem,
        recv_sem=recv_sem,
        device_id=device_at(peer),
        device_id_type=MESH,
    )


def window(ref, fixed, part, dims):
    start, size = COLS[part]
    index = tuple(fixed.get(dim, slice(None)) for dim in dims)
    return ref.at[index + (slice(None), pl.ds(start, size))]


ALL_DIMS = ("x", "core", "y", "z")


def spread_blocks(place, out, send_sem, recv_sem):
    for stage in range(3):
        copies = []
        for part, order in enumerate(ORDERS):
            dim = order[2 - stage]
            fixed = {"core": place["core"]}
            for known in order[: 3 - stage]:
                fixed[known] = place[known]
            block = window(out, fixed, part, ALL_DIMS)
            for step in (1, 2, 3):
                slot = (stage * 3 + part) * 3 + step - 1
                copy = remote(block, block, send_sem.at[slot], recv_sem.at[slot], shifted(place, dim, step))
                copy.start()
                copies.append(copy)
        for copy in copies:
            copy.wait()
    half = out.at[:, place["core"]]
    copy = remote(half, half, send_sem.at[27], recv_sem.at[27], shifted(place, "core", 1))
    copy.start()
    copy.wait()


def gather_kernel(own, out, send_sem, recv_sem):
    place = where_am_i()
    greet(place)
    out[place["x"], place["core"], place["y"], place["z"]] = own[...]
    spread_blocks(place, out, send_sem, recv_sem)


def gather_blocks(own, collective_id):
    rows, width = own.shape
    out = pl.pallas_call(
        gather_kernel,
        out_shape=jax.ShapeDtypeStruct((4, 2, 4, 4, rows, width), own.dtype),
        in_specs=[pl.BlockSpec(memory_space=pltpu.VMEM)],
        out_specs=pl.BlockSpec(memory_space=pltpu.VMEM),
        scratch_shapes=[pltpu.SemaphoreType.DMA((28,)), pltpu.SemaphoreType.DMA((28,))],
        compiler_params=pltpu.CompilerParams(collective_id=collective_id, has_side_effects=True),
        name="gather_blocks",
    )(own)
    return out.reshape(128 * rows, width)


def reduce_kernel(n, *refs):
    sources, refs = refs[:n], refs[n:]
    outs, refs = refs[:2], refs[2:]
    bufs = [refs[i * 7 : i * 7 + 7] for i in range(n)]
    send_sem, recv_sem, ag_send, ag_recv = refs[7 * n :]
    place = where_am_i()
    greet(place)
    f32 = jnp.float32
    partner = shifted(place, "core", 1)
    copies = []
    for i, src in enumerate(sources):
        copy = remote(src.at[:, partner["core"]], bufs[i][0], send_sem.at[i], recv_sem.at[i], partner)
        copy.start()
        copies.append(copy)
    for i, src in enumerate(sources):
        copies[i].wait()
        got, total = bufs[i][0], bufs[i][1]

        def add(t, _, src=src, got=got, total=total):
            x, y, z = t // 16, lax.rem(t // 4, 4), lax.rem(t, 4)
            total[x, y, z] = (src[x, place["core"], y, z].astype(f32) + got[x, y, z].astype(f32)).astype(jnp.bfloat16)
            return 0

        lax.fori_loop(0, 64, add, 0)
    for stage in range(3):
        started = []
        for part, order in enumerate(ORDERS):
            dim = order[stage]
            dims = [d for d in "xyz" if d not in order[:stage]]
            for i in range(n):
                held = bufs[i][1 + 2 * stage]
                came = bufs[i][2 + 2 * stage]
                mine = []
                for step in (1, 2, 3):
                    peer = shifted(place, dim, step)
                    slot = n + ((stage * 3 + part) * n + i) * 3 + step - 1
                    start, size = COLS[part]
                    dst = came.at[(step - 1,) + (slice(None),) * (len(dims) - 1) + (slice(None), pl.ds(start, size))]
                    copy = remote(
                        window(held, {dim: peer[dim]}, part, dims), dst, send_sem.at[slot], recv_sem.at[slot], peer
                    )
                    copy.start()
                    mine.append(copy)
                started.append((part, i, dims, dim, held, came, mine))
        for part, i, dims, dim, held, came, mine in started:
            for copy in mine:
                copy.wait()
            start, size = COLS[part]
            cols = pl.ds(start, size)
            count = 4 ** (len(dims) - 1)

            def fold(t, _, part=part, i=i, dims=dims, dim=dim, held=held, came=came, cols=cols):
                rest = [d for d in dims if d != dim]
                at = {dim: place[dim]}
                if len(rest) == 2:
                    at[rest[0]], at[rest[1]] = t // 4, lax.rem(t, 4)
                elif len(rest) == 1:
                    at[rest[0]] = t
                total = held[tuple(at[d] for d in dims) + (slice(None), cols)].astype(f32)
                for k in range(3):
                    total += came[(k,) + tuple(at[d] for d in rest) + (slice(None), cols)].astype(f32)
                if len(rest):
                    nxt = bufs[i][3 + 2 * stage]
                    nxt[tuple(at[d] for d in rest) + (slice(None), cols)] = total.astype(jnp.bfloat16)
                elif i == 0:
                    outs[0][place["x"], place["core"], place["y"], place["z"], :, cols] = total.astype(jnp.bfloat16)
                else:
                    outs[1][:, cols] = total
                return 0

            if count > 1:
                lax.fori_loop(0, count, fold, 0)
            else:
                fold(0, 0)
    spread_blocks(place, outs[0], ag_send, ag_recv)


def reduce_blocks(grads, hubs, collective_id):
    width = grads.shape[1]
    operands = [a.reshape(4, 2, 4, 4, a.shape[0] // 128, width) for a in (grads, hubs)]
    scratch = []
    for a in operands:
        rows = a.shape[4]
        for shape in (
            (4, 4, 4, rows, width),
            (4, 4, 4, rows, width),
            (3, 4, 4, rows, width),
            (4, 4, rows, width),
            (3, 4, rows, width),
            (4, rows, width),
            (3, rows, width),
        ):
            scratch.append(pltpu.VMEM(shape, jnp.bfloat16))
    n = 2
    count = n + 9 * n * 3
    out, own = pl.pallas_call(
        functools.partial(reduce_kernel, n),
        out_shape=(
            jax.ShapeDtypeStruct(operands[0].shape, jnp.bfloat16),
            jax.ShapeDtypeStruct((operands[1].shape[4], width), jnp.float32),
        ),
        in_specs=[pl.BlockSpec(memory_space=pltpu.VMEM)] * 2,
        out_specs=[pl.BlockSpec(memory_space=pltpu.VMEM)] * 2,
        scratch_shapes=scratch
        + [
            pltpu.SemaphoreType.DMA((count,)),
            pltpu.SemaphoreType.DMA((count,)),
            pltpu.SemaphoreType.DMA((28,)),
            pltpu.SemaphoreType.DMA((28,)),
        ],
        compiler_params=pltpu.CompilerParams(
            collective_id=collective_id, has_side_effects=True, vmem_limit_bytes=48 * 1024 * 1024
        ),
        name="reduce_blocks",
    )(*operands)
    return out.reshape(2048, width), own


def silu_slope(pre_act):
    sigmoid_val = jax.nn.sigmoid(pre_act)
    return sigmoid_val * (1.0 + pre_act * (1.0 - sigmoid_val))


def dot(a, b, ca, cb, kind=jnp.float32):
    return lax.dot_general(a, b, (((ca,), (cb,)), ((), ())), preferred_element_type=kind)


def on_device(
    features, neighbours, degrees, send_rows, send_count, hub_rows, w_self, w_neigh, bias_term, cotangent
):
    n_dev = 128
    n_local, feat_width = features.shape
    fanout = neighbours.shape[1]
    capacity = send_rows.shape[1] // n_dev
    n_slots = n_dev * capacity
    bf16 = jnp.bfloat16
    table_len = n_local + n_slots + hub_rows.shape[0] * n_dev
    slot_live = jnp.arange(capacity, dtype=jnp.int32)[None, :] < send_count.reshape(n_dev, 1)
    live_row = jnp.where(slot_live.reshape(-1), send_rows[0], -1)
    picks = (live_row[:, None] == jnp.arange(n_local, dtype=jnp.int32)[None, :]).astype(bf16)
    outgoing = dot(picks, features, 1, 0, bf16)
    arrived = lax.all_to_all(outgoing, ("row", "col"), split_axis=0, concat_axis=0, tiled=True)
    hub_picks = (hub_rows[:, None] == jnp.arange(n_local, dtype=jnp.int32)[None, :]).astype(bf16)
    own_hubs = dot(hub_picks, features, 1, 0, bf16)
    all_hubs = gather_blocks(own_hubs, 1)

    live = jnp.arange(fanout, dtype=jnp.int32)[None, :] < degrees[:, None]
    target = jnp.where(live, neighbours, -1)
    entry = jnp.arange(table_len, dtype=jnp.int32)[None, :]
    counts = jnp.zeros((n_local, table_len), jnp.float32)
    for j in range(fanout):
        counts += (target[:, j : j + 1] == entry).astype(jnp.float32)
    counts = counts.astype(bf16)
    own_counts = counts[:, :n_local]
    slot_counts = counts[:, n_local : n_local + n_slots]
    hub_counts = counts[:, n_local + n_slots :]
    inv_deg = 1.0 / degrees.astype(jnp.float32)

    summed = dot(own_counts, features, 1, 0) + dot(hub_counts, all_hubs, 1, 0) + dot(slot_counts, arrived, 1, 0)
    aggregate = (summed * inv_deg[:, None]).astype(bf16)
    pre_act = dot(features, w_self, 1, 0) + dot(aggregate, w_neigh, 1, 0) + bias_term[None, :]
    hidden = jax.nn.silu(pre_act).astype(bf16)
    d_pre = (cotangent.astype(jnp.float32) * silu_slope(pre_act)).astype(bf16)

    d_agg = (dot(d_pre, w_neigh, 1, 1) * inv_deg[:, None]).astype(bf16)
    d_arrived = dot(slot_counts, d_agg, 0, 0, bf16)
    returned = lax.all_to_all(d_arrived, ("row", "col"), split_axis=0, concat_axis=0, tiled=True)
    grads = jnp.concatenate([dot(features, d_pre, 0, 0, bf16), dot(aggregate, d_pre, 0, 0, bf16)], 0)
    d_hubs = dot(hub_counts, d_agg, 0, 0, bf16)
    grads, hub_back = reduce_blocks(grads, d_hubs, 2)
    grad_x = dot(d_pre, w_self, 1, 1) + dot(own_counts, d_agg, 0, 0)
    grad_x = grad_x + lax.dot_general(
        hub_picks.astype(jnp.float32),
        hub_back,
        (((0,), (0,)), ((), ())),
        precision=lax.Precision.HIGHEST,
        preferred_element_type=jnp.float32,
    )
    grad_x = grad_x + dot(picks, returned, 0, 0)
    return (hidden, grad_x.astype(bf16), grads[:feat_width], grads[feat_width:])


def solution(mesh):
    split = P(("row", "col"), None)
    in_specs = (split, split, P(("row", "col")), split, split, P(("row", "col")), P(), P(), P(), split)
    out_specs = (split, split, P(), P())
    return jax.shard_map(on_device, mesh=mesh, in_specs=in_specs, out_specs=out_specs, check_vma=False)
```

```python
import functools

import jax
import jax.numpy as jnp
from jax import lax
from jax.experimental import pallas as pl
from jax.experimental.pallas import tpu as pltpu
from jax.sharding import PartitionSpec as P

MESH = pl.DeviceIdType.MESH
F32 = jnp.float32
BF16 = jnp.bfloat16
WIDTH = 1024
LOCAL = 512
FANOUT = 16
SLOT = 16
HUB = 8
PEERS = 128
SLOTS = SLOT * PEERS
HUBS = HUB * PEERS
TABLE = LOCAL + SLOTS + HUBS
STRIDE = 37
COLS = ((0, 384), (384, 384), (768, 256))
ORDERS = (("x", "y", "z"), ("y", "z", "x"), ("z", "x", "y"))
ALL_DIMS = ("x", "core", "y", "z")


def where_am_i():
    row = lax.axis_index("row")
    col = lax.axis_index("col")
    return {"x": row // 2, "core": lax.rem(row, 2), "y": col // 4, "z": lax.rem(col, 4)}


def device_at(place):
    return (place["x"] * 2 + place["core"], place["y"] * 4 + place["z"])


def rank_of(place):
    return ((place["x"] * 2 + place["core"]) * 4 + place["y"]) * 4 + place["z"]


def shifted(place, dim, step):
    other = dict(place)
    other[dim] = lax.rem(place[dim] + step, 2 if dim == "core" else 4)
    return other


def peer_at(place, offset):
    return {
        "x": lax.rem(place["x"] + offset // 32, 4),
        "core": lax.rem(place["core"] + lax.rem(offset // 16, 2), 2),
        "y": lax.rem(place["y"] + lax.rem(offset // 4, 4), 4),
        "z": lax.rem(place["z"] + lax.rem(offset, 4), 4),
    }


def remote(src, dst, send_sem, recv_sem, peer):
    return pltpu.make_async_remote_copy(
        src_ref=src,
        dst_ref=dst,
        send_sem=send_sem,
        recv_sem=recv_sem,
        device_id=device_at(peer),
        device_id_type=MESH,
    )


def dot(a, b, ca=1, cb=0):
    return lax.dot_general(a, b, (((ca,), (cb,)), ((), ())), preferred_element_type=F32)


def loop(count, body):
    def step(i, carry):
        body(i)
        return carry

    lax.fori_loop(0, count, step, 0)


def rows(i, size):
    return pl.ds(pl.multiple_of(i * size, size), size)


def cut(part):
    start, size = COLS[part]
    return pl.ds(start, size)


def window(ref, fixed, part, dims):
    index = tuple(fixed.get(dim, slice(None)) for dim in dims)
    return ref.at[index + (slice(None), cut(part))]


class Exchange:
    def __init__(self, place, src, dst, send_sem, recv_sem):
        self.place, self.src, self.dst = place, src, dst
        self.send_sem, self.recv_sem = send_sem, recv_sem
        self.me = rank_of(place)

    def send(self, low, high):
        def body(i):
            peer = peer_at(self.place, lax.rem((low + i) * STRIDE, PEERS))
            remote(
                self.src.at[rows(rank_of(peer), SLOT)],
                self.dst.at[rows(self.me, SLOT)],
                self.send_sem,
                self.recv_sem,
                peer,
            ).start()

        loop(high - low, body)

    def wait_recv(self):
        most = pl.ds(0, SLOTS - SLOT)
        pltpu.make_async_copy(self.src.at[most], self.dst.at[most], self.recv_sem).wait()

    def wait_send(self):
        most = pl.ds(0, SLOTS - SLOT)
        pltpu.make_async_copy(self.src.at[most], self.dst.at[most], self.send_sem).wait()


class Spread:
    def __init__(self, place, out, send_sem, recv_sem):
        self.place, self.out, self.send_sem, self.recv_sem = place, out, send_sem, recv_sem

    def start(self, stage):
        place, out = self.place, self.out
        self.copies = []
        if stage == 3:
            half = out.at[:, place["core"]]
            self.copies.append(
                remote(half, half, self.send_sem.at[27], self.recv_sem.at[27], shifted(place, "core", 1))
            )
        else:
            for part, order in enumerate(ORDERS):
                dim = order[2 - stage]
                fixed = {"core": place["core"]}
                for known in order[: 3 - stage]:
                    fixed[known] = place[known]
                block = window(out, fixed, part, ALL_DIMS)
                for step in (2, 1, 3):
                    slot = (stage * 3 + part) * 3 + step - 1
                    self.copies.append(
                        remote(block, block, self.send_sem.at[slot], self.recv_sem.at[slot], shifted(place, dim, step))
                    )
        for copy in self.copies:
            copy.start()

    def finish(self):
        for copy in self.copies:
            copy.wait()


class Reduce:
    def __init__(self, place, sources, bufs, finals, send_sem, recv_sem):
        self.place, self.sources, self.bufs, self.finals = place, sources, bufs, finals
        self.send_sem, self.recv_sem = send_sem, recv_sem

    def start_core(self):
        partner = shifted(self.place, "core", 1)
        self.copies = []
        for i, src in enumerate(self.sources):
            copy = remote(
                src.at[:, partner["core"]], self.bufs[i][0], self.send_sem.at[i], self.recv_sem.at[i], partner
            )
            copy.start()
            self.copies.append(copy)

    def finish_core(self):
        core = self.place["core"]
        for i, src in enumerate(self.sources):
            self.copies[i].wait()
            got, total = self.bufs[i][0], self.bufs[i][1]

            def add(t, src=src, got=got, total=total):
                x, y, z = t // 16, lax.rem(t // 4, 4), lax.rem(t, 4)
                total[x, y, z] = (src[x, core, y, z].astype(F32) + got[x, y, z].astype(F32)).astype(BF16)

            loop(64, add)

    def start(self, stage):
        place, n = self.place, len(self.sources)
        self.started = []
        for part, order in enumerate(ORDERS):
            dim = order[stage]
            dims = [d for d in "xyz" if d not in order[:stage]]
            for i in range(n):
                held, came = self.bufs[i][1 + 2 * stage], self.bufs[i][2 + 2 * stage]
                mine = []
                for step in (2, 1, 3):
                    peer = shifted(place, dim, step)
                    slot = n + ((stage * 3 + part) * n + i) * 3 + step - 1
                    dst = came.at[(step - 1,) + (slice(None),) * (len(dims) - 1) + (slice(None), cut(part))]
                    copy = remote(
                        window(held, {dim: peer[dim]}, part, dims),
                        dst,
                        self.send_sem.at[slot],
                        self.recv_sem.at[slot],
                        peer,
                    )
                    copy.start()
                    mine.append(copy)
                self.started.append((part, i, dims, dim, held, came, mine))

    def finish(self, stage):
        place = self.place
        for part, i, dims, dim, held, came, mine in self.started:
            for copy in mine:
                copy.wait()
            cols = cut(part)
            rest = [d for d in dims if d != dim]

            def fold(t, part=part, i=i, dims=dims, dim=dim, held=held, came=came, cols=cols, rest=rest):
                at = {dim: place[dim]}
                if len(rest) == 2:
                    at[rest[0]], at[rest[1]] = t // 4, lax.rem(t, 4)
                elif len(rest) == 1:
                    at[rest[0]] = t
                spot = tuple(at[d] for d in rest)
                total = held[tuple(at[d] for d in dims) + (slice(None), cols)].astype(F32)
                for k in range(3):
                    total += came[(k,) + spot + (slice(None), cols)].astype(F32)
                if rest:
                    self.bufs[i][3 + 2 * stage][spot + (slice(None), cols)] = total.astype(BF16)
                else:
                    self.finals[i](cols, total)

            if rest:
                loop(4 ** len(rest), fold)
            else:
                fold(0)


def sage_kernel(
    features,
    neighbours_t,
    degrees,
    send_rows,
    send_count,
    hub_rows,
    bias,
    w_self_hbm,
    w_neigh_hbm,
    cotangent_hbm,
    hidden,
    grad_x,
    grads_all,
    w_self,
    w_neigh,
    cotangent,
    picks_t,
    hub_picks,
    outgoing,
    arrived,
    returned,
    hub_blocks,
    hub_table,
    nbr_wide,
    counts_t,
    counts,
    inv_deg,
    total,
    pre_self,
    aggregate,
    d_pre,
    d_agg,
    grads_own,
    hubs_own,
    hub_back,
    *rest,
):
    bufs = [rest[0:7], rest[7:14]]
    (
        local_sem,
        fwd_send,
        fwd_recv,
        bwd_send,
        bwd_recv,
        hub_send,
        hub_recv,
        red_send,
        red_recv,
        all_send,
        all_recv,
    ) = rest[14:]
    place = where_am_i()
    me = rank_of(place)
    barrier = pltpu.get_barrier_semaphore()

    def greet(i):
        peer = peer_at(place, i + 1)
        pl.semaphore_signal(barrier, inc=1, device_id=device_at(peer), device_id_type=MESH)

    loop(PEERS - 1, greet)
    loads = [
        pltpu.make_async_copy(src, dst, local_sem.at[i])
        for i, (src, dst) in enumerate(((w_self_hbm, w_self), (w_neigh_hbm, w_neigh), (cotangent_hbm, cotangent)))
    ]
    for load in loads:
        load.start()

    owner = lax.broadcasted_iota(jnp.int32, (PEERS, SLOTS), 1) // SLOT
    widen = (owner == lax.broadcasted_iota(jnp.int32, (PEERS, SLOTS), 0)).astype(F32).astype(BF16)
    count = jnp.broadcast_to(send_count[...], (8, PEERS)).astype(F32).astype(BF16)
    count_wide = dot(count, widen)[0:1]
    place_in = lax.rem(lax.broadcasted_iota(jnp.int32, (1, SLOTS), 1), SLOT)
    live_row = jnp.where(place_in.astype(F32) < count_wide, send_rows[...], -1)

    def pick(i):
        row = lax.broadcasted_iota(jnp.int32, (64, SLOTS), 0) + i * 64
        picks_t[rows(i, 64)] = (row == live_row).astype(F32).astype(BF16)

    loop(LOCAL // 64, pick)

    def fill(i):
        outgoing[rows(i, 512)] = dot(picks_t[:, rows(i, 512)], features[...], 0, 0).astype(BF16)

    loop(SLOTS // 512, fill)
    which = lax.broadcasted_iota(jnp.int32, (SLOT, LOCAL), 0)
    chosen = jnp.zeros((SLOT, LOCAL), jnp.int32)
    for h in range(HUB):
        chosen = jnp.where(lax.rem(which, HUB) == h, hub_rows[h], chosen)
    hub_picks[...] = (chosen == lax.broadcasted_iota(jnp.int32, (SLOT, LOCAL), 1)).astype(F32).astype(BF16)
    own_hubs = dot(hub_picks[...], features[...])[:HUB]
    hub_blocks[place["x"], place["core"], place["y"], place["z"]] = own_hubs.astype(BF16)
    arrived[rows(me, SLOT)] = jnp.zeros((SLOT, WIDTH), BF16)
    returned[rows(me, SLOT)] = jnp.zeros((SLOT, WIDTH), BF16)

    forward = Exchange(place, outgoing, arrived, fwd_send, fwd_recv)
    backward = Exchange(place, outgoing, returned, bwd_send, bwd_recv)
    hub_spread = Spread(place, hub_blocks, hub_send, hub_recv)
    pl.semaphore_wait(barrier, PEERS - 1)

    live = lax.broadcasted_iota(jnp.int32, (FANOUT, LOCAL), 0) < degrees[...]
    target = jnp.where(live, neighbours_t[...], -1)
    for j in range(FANOUT):
        nbr_wide[j] = jnp.broadcast_to(target[j : j + 1], (8, LOCAL))
    inv_deg[...] = (1.0 / jnp.broadcast_to(degrees[...], (128, LOCAL)).astype(F32)).T

    def count_block(b):
        def strip(i):
            base = b * 128 + i * 32
            sums = [jnp.zeros((8, LOCAL), F32) for _ in range(4)]
            ids = [lax.broadcasted_iota(jnp.int32, (8, LOCAL), 0) + (base + 8 * g) for g in range(4)]
            for j in range(FANOUT):
                named = nbr_wide[j]
                for g in range(4):
                    sums[g] = sums[g] + jnp.where(named == ids[g], 1.0, 0.0)
            counts_t[pl.ds(pl.multiple_of(base, 32), 32)] = jnp.concatenate(sums, 0).astype(BF16)

        loop(4, strip)
        counts[:, rows(b, 128)] = counts_t[rows(b, 128)].astype(F32).T.astype(BF16)

    blocks = TABLE // 128
    for stage in range(4):
        hub_spread.start(stage)
        forward.send(1 + stage * 32, min(1 + (stage + 1) * 32, PEERS))
        first = blocks * stage // 4
        loop(blocks * (stage + 1) // 4 - first, lambda i, first=first: count_block(first + i))
        hub_spread.finish()

    def to_table(x):
        hub_table[rows(x, 256)] = hub_blocks[x].astype(F32).reshape(256, WIDTH).astype(BF16)

    loop(4, to_table)
    loads[0].wait()

    def before(i):
        cols = rows(i, 256)
        pre_self[:, cols] = dot(features[...], w_self[:, cols]) + bias[:, cols]
        total[:, cols] = dot(counts[:, :LOCAL], features[:, cols]) + dot(
            counts[:, LOCAL + SLOTS :], hub_table[:, cols]
        )

    loop(4, before)
    loads[1].wait()
    loads[2].wait()
    forward.wait_recv()

    def with_slots(i):
        cols = rows(i, 256)
        total[:, cols] += dot(counts[:, LOCAL : LOCAL + SLOTS], arrived[:, cols])

    loop(4, with_slots)

    def mean(i):
        scale = jnp.concatenate([inv_deg[rows(i, 64)]] * (WIDTH // 128), 1)
        aggregate[rows(i, 64)] = (total[rows(i, 64)] * scale).astype(BF16)

    loop(LOCAL // 64, mean)

    def act(i):
        m = rows(i, 128)
        pre = pre_self[m] + dot(aggregate[m], w_neigh[...])
        sigmoid = jax.nn.sigmoid(pre)
        hidden[m] = (pre * sigmoid).astype(BF16)
        slope = sigmoid * (1.0 + pre * (1.0 - sigmoid))
        d_pre[m] = (cotangent[m].astype(F32) * slope).astype(BF16)

    loop(LOCAL // 128, act)

    def d_mean(i):
        m = rows(i, 128)
        scale = jnp.concatenate([inv_deg[m]] * (WIDTH // 128), 1)
        d_agg[m] = (dot(d_pre[m], w_neigh[...], 1, 1) * scale).astype(BF16)

    loop(LOCAL // 128, d_mean)
    forward.wait_send()

    def d_slots(i):
        m = rows(i, 512)
        outgoing[m] = dot(counts_t[pl.ds(pl.multiple_of(LOCAL + i * 512, 512), 512)], d_agg[...]).astype(BF16)

    loop(SLOTS // 512, d_slots)
    backward.send(1, 25)

    def grads_to(first, source):
        def body(i):
            block = dot(source[:, rows(i, 512)], d_pre[...], 0, 0).astype(BF16)
            grads_own[first + i] = block.reshape(2, 4, 4, SLOT, WIDTH)

        loop(2, body)

    grads_to(0, features)
    grads_to(2, aggregate)

    def d_hubs(i):
        base = LOCAL + SLOTS + i * 256
        block = dot(counts_t[pl.ds(pl.multiple_of(base, 256), 256)], d_agg[...])
        hubs_own[i] = block.reshape(2, 4, 4, HUB, WIDTH).astype(BF16)

    loop(4, d_hubs)

    def keep_grads(cols, value):
        grads_all[place["x"], place["core"], place["y"], place["z"], :, cols] = value.astype(BF16)

    def keep_hubs(cols, value):
        hub_back[:, cols] = value

    reduce = Reduce(place, (grads_own, hubs_own), bufs, (keep_grads, keep_hubs), red_send, red_recv)
    spread = Spread(place, grads_all, all_send, all_recv)
    reduce.start_core()
    backward.send(25, 42)

    def own_grad(i):
        m = rows(i, 128)
        total[m] = dot(d_pre[m], w_self[...], 1, 1) + dot(counts_t[m], d_agg[...])

    loop(LOCAL // 128, own_grad)
    reduce.finish_core()
    reduce.start(0)
    backward.send(42, 62)
    reduce.finish(0)
    reduce.start(1)
    backward.send(62, 80)
    reduce.finish(1)
    reduce.start(2)
    backward.send(80, 96)
    reduce.finish(2)
    spread.start(0)
    backward.send(96, 112)
    spread.finish()
    spread.start(1)
    backward.send(112, PEERS)
    spread.finish()
    spread.start(2)

    high = hub_back[...].astype(BF16)
    low = (hub_back[...] - high.astype(F32)).astype(BF16)
    both = jnp.concatenate([high.astype(F32), low.astype(F32)], 0).astype(BF16)
    backward.wait_recv()

    def final(i):
        cols = rows(i, 256)
        value = total[:, cols] + dot(picks_t[...], returned[:, cols])
        total[:, cols] = value

    loop(4, final)
    grad_x[...] = (total[...] + dot(hub_picks[...], both, 0, 0)).astype(BF16)
    spread.finish()
    spread.start(3)
    backward.wait_send()
    spread.finish()


def on_device(
    features, neighbours, degrees, send_rows, send_count, hub_rows, w_self, w_neigh, bias_term, cotangent
):
    vmem = pl.BlockSpec(memory_space=pltpu.VMEM)
    hbm = pl.BlockSpec(memory_space=pl.ANY)
    wide = (WIDTH,)

    def buf(*shape, kind=BF16):
        return pltpu.VMEM(shape, kind)

    reduce_bufs = []
    for size in (SLOT, HUB):
        for shape in ((4, 4, 4), (4, 4, 4), (3, 4, 4), (4, 4), (3, 4), (4,), (3,)):
            reduce_bufs.append(buf(*shape, size, WIDTH))
    dma = pltpu.SemaphoreType.DMA
    hidden, grad_x, grads = pl.pallas_call(
        sage_kernel,
        out_shape=(
            jax.ShapeDtypeStruct((LOCAL, WIDTH), BF16),
            jax.ShapeDtypeStruct((LOCAL, WIDTH), BF16),
            jax.ShapeDtypeStruct((4, 2, 4, 4, SLOT, WIDTH), BF16),
        ),
        in_specs=[vmem] * 5 + [pl.BlockSpec(memory_space=pltpu.SMEM)] + [vmem] + [hbm] * 3,
        out_specs=[vmem] * 3,
        scratch_shapes=[
            buf(WIDTH, WIDTH),
            buf(WIDTH, WIDTH),
            buf(LOCAL, WIDTH),
            buf(LOCAL, SLOTS),
            buf(SLOT, LOCAL),
            buf(SLOTS, WIDTH),
            buf(SLOTS, WIDTH),
            buf(SLOTS, WIDTH),
            buf(4, 2, 4, 4, HUB, WIDTH),
            buf(HUBS, WIDTH),
            buf(FANOUT, 8, LOCAL, kind=jnp.int32),
            buf(TABLE, LOCAL),
            buf(LOCAL, TABLE),
            buf(LOCAL, 128, kind=F32),
            buf(LOCAL, WIDTH, kind=F32),
            buf(LOCAL, WIDTH, kind=F32),
            buf(LOCAL, WIDTH),
            buf(LOCAL, WIDTH),
            buf(LOCAL, WIDTH),
            buf(4, 2, 4, 4, SLOT, WIDTH),
            buf(4, 2, 4, 4, HUB, WIDTH),
            buf(HUB, WIDTH, kind=F32),
            *reduce_bufs,
            dma((3,)),
            dma,
            dma,
            dma,
            dma,
            dma((28,)),
            dma((28,)),
            dma((56,)),
            dma((56,)),
            dma((28,)),
            dma((28,)),
        ],
        compiler_params=pltpu.CompilerParams(
            collective_id=0, has_side_effects=True, vmem_limit_bytes=67043328
        ),
        name="sage",
    )(
        features,
        neighbours.T,
        degrees[None, :],
        send_rows,
        send_count,
        hub_rows,
        bias_term[None, :],
        w_self,
        w_neigh,
        cotangent,
    )
    grads = grads.reshape(2 * WIDTH, WIDTH)
    return hidden, grad_x, grads[:WIDTH], grads[WIDTH:]


def solution(mesh):
    split = P(("row", "col"), None)
    in_specs = (split, split, P(("row", "col")), split, split, P(("row", "col")), P(), P(), P(), split)
    out_specs = (split, split, P(), P())
    return jax.shard_map(on_device, mesh=mesh, in_specs=in_specs, out_specs=out_specs, check_vma=False)
```

```python
import functools

import jax
import jax.numpy as jnp
from jax import lax
from jax.experimental import pallas as pl
from jax.experimental.pallas import tpu as pltpu
from jax.sharding import PartitionSpec as P

MESH = pl.DeviceIdType.MESH
F32 = jnp.float32
BF16 = jnp.bfloat16
WIDTH = 1024
LOCAL = 512
FANOUT = 16
SLOT = 16
HUB = 8
PEERS = 128
SLOTS = SLOT * PEERS
HUBS = HUB * PEERS
TABLE = LOCAL + SLOTS + HUBS
XYZ, YZX, ZXY = ("x", "y", "z"), ("y", "z", "x"), ("z", "x", "y")
HUB_PIECES = ((0, 0, 384, XYZ), (0, 384, 384, YZX), (0, 768, 256, ZXY))
GRAD_PIECES = ((0, 0, 640, XYZ), (1, 0, 640, YZX), (0, 640, 384, ZXY), (1, 640, 384, ZXY))
SUM_ORDERS = (XYZ, YZX, ZXY)


def where_am_i():
    row = lax.axis_index("row")
    col = lax.axis_index("col")
    return {"x": row // 2, "core": lax.rem(row, 2), "y": col // 4, "z": lax.rem(col, 4)}


def device_at(place):
    return (place["x"] * 2 + place["core"], place["y"] * 4 + place["z"])


def rank_of(place):
    return ((place["x"] * 2 + place["core"]) * 4 + place["y"]) * 4 + place["z"]


def shifted(place, dim, step):
    other = dict(place)
    other[dim] = lax.rem(place[dim] + step, 2 if dim == "core" else 4)
    return other


def message_order():
    left = [(x, c, y, z) for x in range(4) for y in range(4) for z in range(4) for c in range(2)][1:]
    load = [0] * 6
    order = []

    def after(offset):
        new = list(load)
        for axis, step in enumerate((offset[0], offset[2], offset[3])):
            if step in (1, 2):
                new[2 * axis] += 1
            if step in (2, 3):
                new[2 * axis + 1] += 1
        return new

    def unevenness(offset):
        new = after(offset)
        mean = sum(new) / 6
        return (max(new) - min(new), sum((v - mean) ** 2 for v in new), [(7 * v) % 4 for v in offset])

    while left:
        best = min(left, key=unevenness)
        left.remove(best)
        load[:] = after(best)
        order.append(best)
    return order


ORDER = message_order()


class Peers:
    def __init__(self, place):
        xs = [lax.rem(place["x"] + d, 4) for d in range(4)]
        cores = [place["core"], 1 - place["core"]]
        ys = [lax.rem(place["y"] + d, 4) for d in range(4)]
        zs = [lax.rem(place["z"] + d, 4) for d in range(4)]
        self.rows = [[x * 2 + c for c in cores] for x in xs]
        self.cols = [[y * 4 + z for z in zs] for y in ys]

    def device(self, offset):
        return (self.rows[offset[0]][offset[1]], self.cols[offset[2]][offset[3]])

    def rank(self, offset):
        row, col = self.device(offset)
        return row * 16 + col


def remote(src, dst, send_sem, recv_sem, peer):
    return pltpu.make_async_remote_copy(
        src_ref=src,
        dst_ref=dst,
        send_sem=send_sem,
        recv_sem=recv_sem,
        device_id=device_at(peer),
        device_id_type=MESH,
    )


def dot(a, b, ca=1, cb=0):
    return lax.dot_general(a, b, (((ca,), (cb,)), ((), ())), preferred_element_type=F32)


def loop(count, body):
    def step(i, carry):
        body(i)
        return carry

    lax.fori_loop(0, count, step, 0)


def rows(i, size):
    return pl.ds(pl.multiple_of(i * size, size), size)


PLANE = [(i, j) for i in range(4) for j in range(4)][1:]


def in_plane(place, order, steps):
    return shifted(shifted(place, order[1], steps[0]), order[2], steps[1])


def wait_for(ref, slot, send_sem, recv_sem):
    for sem in (send_sem, recv_sem):
        pltpu.make_async_copy(ref, ref, sem.at[slot]).wait()


class Exchange:
    def __init__(self, peers, me, src, dst, send_sem, recv_sem):
        self.peers, self.me, self.src, self.dst = peers, me, src, dst
        self.send_sem, self.recv_sem = send_sem, recv_sem
        self.sent = 0

    def send(self, count=PEERS):
        for offset in ORDER[self.sent : self.sent + count]:
            pltpu.make_async_remote_copy(
                src_ref=self.src.at[rows(self.peers.rank(offset), SLOT)],
                dst_ref=self.dst.at[rows(self.me, SLOT)],
                send_sem=self.send_sem,
                recv_sem=self.recv_sem,
                device_id=self.peers.device(offset),
                device_id_type=MESH,
            ).start()
        self.sent += count

    def wait_recv(self):
        most = pl.ds(0, SLOTS - SLOT)
        pltpu.make_async_copy(self.src.at[most], self.dst.at[most], self.recv_sem).wait()

    def wait_send(self):
        most = pl.ds(0, SLOTS - SLOT)
        pltpu.make_async_copy(self.src.at[most], self.dst.at[most], self.send_sem).wait()


class Spread:
    def __init__(self, place, outs, orders, sizes, send_sem, recv_sem):
        self.place, self.outs, self.orders, self.sizes = place, outs, orders, sizes
        self.send_sem, self.recv_sem = send_sem, recv_sem
        self.passed = []

    def send(self, piece, spot, kind, peer):
        block = self.outs[piece].at[(self.place["core"],) + spot]
        slot = piece * 10 + kind
        copy = remote(block, block, self.send_sem.at[slot], self.recv_sem.at[slot], peer)
        copy.start()
        return copy

    def hand_over(self, piece, spot, kind):
        self.passed.append(self.send(piece, spot, kind, shifted(self.place, "core", 1)))

    def start_plane(self):
        for steps in PLANE:
            for piece, order in enumerate(self.orders):
                spot = tuple(self.place[d] for d in order)
                self.send(piece, spot, 9, in_plane(self.place, order, steps))

    def finish_plane(self):
        for piece, size in enumerate(self.sizes):
            wait_for(size.at[:, :, : self.outs[piece].shape[-1]], piece * 10 + 9, self.send_sem, self.recv_sem)

    def start_last(self):
        self.copies = []
        for piece, order in enumerate(self.orders):
            spot = (self.place[order[0]],)
            up = self.send(piece, spot, 0, shifted(self.place, order[0], 1))
            down = self.send(piece, spot, 1, shifted(self.place, order[0], 3))
            self.copies.append((up, down))
        for piece, order in enumerate(self.orders):
            self.hand_over(piece, (self.place[order[0]],), 4)

    def relay(self):
        relayed = []
        for piece, order in enumerate(self.orders):
            at, (up, down) = self.place[order[0]], self.copies[piece]
            below, above = lax.rem(at + 3, 4), lax.rem(at + 1, 4)
            up.wait()
            first = self.send(piece, (below, pl.ds(0, 2)), 2, shifted(self.place, order[0], 1))
            self.hand_over(piece, (below,), 5)
            down.wait()
            second = self.send(piece, (above, pl.ds(2, 2)), 3, shifted(self.place, order[0], 3))
            self.hand_over(piece, (above,), 6)
            relayed.append((first, second))
        self.copies = relayed

    def finish_last(self):
        for piece, order in enumerate(self.orders):
            far = lax.rem(self.place[order[0]] + 2, 4)
            for half, copy in enumerate(self.copies[piece]):
                copy.wait()
                self.hand_over(piece, (far, pl.ds(2 * half, 2)), 7 + half)

    def finish_cores(self):
        for copy in self.passed:
            copy.wait()


class Reduce:
    def __init__(self, place, own, got, held, half, near, came, final, send_sem, recv_sem):
        self.place, self.own, self.got, self.held = place, own, got, held
        self.half, self.near, self.came, self.final = half, near, came, final
        self.send_sem, self.recv_sem = send_sem, recv_sem

    def send(self, src, dst, slot, peer):
        copy = remote(src, dst, self.send_sem.at[slot], self.recv_sem.at[slot], peer)
        copy.start()
        return copy

    def start_core(self, source):
        partner = shifted(self.place, "core", 1)
        return self.send(self.own[source].at[partner["core"]], self.got[source], source, partner)

    def finish_core(self, source, copy):
        core = self.place["core"]
        own, got, held = self.own[source], self.got[source], self.held[0][source]
        copy.wait()

        def add(t):
            a, b = t // 4, lax.rem(t, 4)
            held[a, b] = (own[core, a, b].astype(F32) + got[a, b].astype(F32)).astype(BF16)

        loop(16, add)

    def start_halves(self):
        self.copies = []
        for source, order in enumerate(SUM_ORDERS):
            far = lax.rem(self.place[order[0]] + 2, 4)
            for i, step in enumerate((1, 3)):
                part = self.held[0][source].at[far, pl.ds(2 * i, 2)]
                peer = shifted(self.place, order[0], step)
                self.copies.append(self.send(part, self.half[source].at[i], 3 + source * 2 + i, peer))

    def finish_halves(self):
        for source, order in enumerate(SUM_ORDERS):
            held, half = self.held[0][source], self.half[source]
            for i, step in enumerate((1, 3)):
                self.copies[source * 2 + i].wait()
                at = lax.rem(self.place[order[0]] + step, 4)
                for b in range(2):
                    value = held[at, 2 * i + b].astype(F32) + half[i, b].astype(F32)
                    held[at, 2 * i + b] = value.astype(BF16)

    def start_near(self):
        self.copies = []
        for source, order in enumerate(SUM_ORDERS):
            for i, step in enumerate((1, 3)):
                peer = shifted(self.place, order[0], step)
                part = self.held[0][source].at[peer[order[0]]]
                self.copies.append(self.send(part, self.near[source].at[i], 9 + source * 2 + i, peer))

    def finish_near(self):
        for source, order in enumerate(SUM_ORDERS):
            for i in range(2):
                self.copies[source * 2 + i].wait()
            held, near, at = self.held[0][source], self.near[source], self.place[order[0]]

            def fold(b, source=source, held=held, near=near, at=at):
                value = held[at, b].astype(F32) + near[0, b].astype(F32) + near[1, b].astype(F32)
                self.held[1][source][b] = value.astype(BF16)

            loop(4, fold)

    def start_plane(self):
        for k, steps in enumerate(PLANE):
            for source, order in enumerate(SUM_ORDERS):
                peer = in_plane(self.place, order, steps)
                part = self.held[1][source].at[peer[order[1]], peer[order[2]]]
                self.send(part, self.came[source].at[k], 15 + source, peer)

    def finish_plane(self):
        for source in range(3):
            wait_for(self.came[source], 15 + source, self.send_sem, self.recv_sem)
        for source, order in enumerate(SUM_ORDERS):
            value = self.held[1][source][self.place[order[1]], self.place[order[2]]].astype(F32)
            for k in range(15):
                value += self.came[source][k].astype(F32)
            self.final(source, value)


def sage_kernel(
    features,
    neighbours_t,
    degrees,
    send_rows,
    send_count,
    hub_rows,
    bias,
    w_self_hbm,
    w_neigh_hbm,
    cotangent_hbm,
    hidden_hbm,
    grad_x_hbm,
    all_self,
    all_neigh,
    hidden,
    grad_x,
    w_self,
    w_neigh,
    w_neigh_t,
    cotangent,
    picks_t,
    hub_picks,
    outgoing,
    arrived,
    returned,
    hub_table,
    nbr_wide,
    counts_t,
    counts,
    inv_deg,
    total,
    pre_self,
    aggregate,
    d_pre,
    d_agg,
    hub_back,
    *rest,
):
    groups, at = [], 0
    for size in (3, 4, 3, 3, 3, 3, 3, 3, 3):
        groups.append(rest[at : at + size])
        at += size
    hub_parts, all_parts, own, got, *held, half, near, came = groups
    (
        local_sem,
        out_sem,
        fwd_send,
        fwd_recv,
        bwd_send,
        bwd_recv,
        hub_send,
        hub_recv,
        red_send,
        red_recv,
        all_send,
        all_recv,
    ) = rest[28:]
    place = where_am_i()
    me = rank_of(place)
    barrier = pltpu.get_barrier_semaphore()

    peers = Peers(place)
    for offset in sorted(ORDER, key=lambda o: -sum(min(o[i], 4 - o[i]) for i in (0, 2, 3))):
        pl.semaphore_signal(barrier, inc=1, device_id=peers.device(offset), device_id_type=MESH)
    loads = [
        pltpu.make_async_copy(src, dst, local_sem.at[i])
        for i, (src, dst) in enumerate(((w_self_hbm, w_self), (w_neigh_hbm, w_neigh), (cotangent_hbm, cotangent)))
    ]
    for load in loads:
        load.start()

    owner = lax.broadcasted_iota(jnp.int32, (PEERS, SLOTS), 1) // SLOT
    widen = (owner == lax.broadcasted_iota(jnp.int32, (PEERS, SLOTS), 0)).astype(F32).astype(BF16)
    count = jnp.broadcast_to(send_count[...], (8, PEERS)).astype(F32).astype(BF16)
    count_wide = dot(count, widen)[0:1]
    place_in = lax.rem(lax.broadcasted_iota(jnp.int32, (1, SLOTS), 1), SLOT)
    live_row = jnp.where(place_in.astype(F32) < count_wide, send_rows[...], -1)

    def pick(i):
        row = lax.broadcasted_iota(jnp.int32, (64, SLOTS), 0) + i * 64
        picks_t[rows(i, 64)] = (row == live_row).astype(F32).astype(BF16)

    loop(LOCAL // 64, pick)

    def fill(i):
        outgoing[rows(i, 512)] = dot(picks_t[:, rows(i, 512)], features[...], 0, 0).astype(BF16)

    loop(SLOTS // 512, fill)
    which = lax.broadcasted_iota(jnp.int32, (SLOT, LOCAL), 0)
    chosen = jnp.zeros((SLOT, LOCAL), jnp.int32)
    for h in range(HUB):
        chosen = jnp.where(lax.rem(which, HUB) == h, hub_rows[h], chosen)
    hub_picks[...] = (chosen == lax.broadcasted_iota(jnp.int32, (SLOT, LOCAL), 1)).astype(F32).astype(BF16)
    own_hubs = dot(hub_picks[...], features[...])[:HUB]
    for part, (_, start, size, order) in zip(hub_parts, HUB_PIECES):
        part[(place["core"],) + tuple(place[d] for d in order)] = own_hubs[:, start : start + size].astype(BF16)
    arrived[rows(me, SLOT)] = jnp.zeros((SLOT, WIDTH), BF16)
    returned[rows(me, SLOT)] = jnp.zeros((SLOT, WIDTH), BF16)

    forward = Exchange(peers, me, outgoing, arrived, fwd_send, fwd_recv)
    backward = Exchange(peers, me, outgoing, returned, bwd_send, bwd_recv)
    hub_spread = Spread(place, hub_parts, [p[3] for p in HUB_PIECES], [came[0]] * 3, hub_send, hub_recv)
    pl.semaphore_wait(barrier, PEERS - 1)

    live = lax.broadcasted_iota(jnp.int32, (FANOUT, LOCAL), 0) < degrees[...]
    target = jnp.where(live, neighbours_t[...], -1)
    for j in range(FANOUT):
        nbr_wide[j] = jnp.broadcast_to(target[j : j + 1], (8, LOCAL))
    inv_deg[...] = (1.0 / jnp.broadcast_to(degrees[...], (128, LOCAL)).astype(F32)).T

    def count_block(b):
        def strip(i):
            base = b * 128 + i * 32
            sums = [jnp.zeros((8, LOCAL), F32) for _ in range(4)]
            ids = [lax.broadcasted_iota(jnp.int32, (8, LOCAL), 0) + (base + 8 * g) for g in range(4)]
            for j in range(FANOUT):
                named = nbr_wide[j]
                for g in range(4):
                    sums[g] = sums[g] + jnp.where(named == ids[g], 1.0, 0.0)
            counts_t[pl.ds(pl.multiple_of(base, 32), 32)] = jnp.concatenate(sums, 0).astype(BF16)

        loop(4, strip)
        counts[:, rows(b, 128)] = counts_t[rows(b, 128)].astype(F32).T.astype(BF16)

    def count_blocks(low, high):
        loop(high - low, lambda i: count_block(low + i))

    hub_spread.start_plane()
    forward.send(30)
    count_blocks(0, 14)
    hub_spread.finish_plane()
    hub_spread.start_last()
    forward.send(40)
    count_blocks(14, 21)
    hub_spread.relay()
    forward.send()
    count_blocks(21, 28)
    hub_spread.finish_last()

    loads[1].wait()

    def turn(i):
        w_neigh_t[:, rows(i, 128)] = w_neigh[rows(i, 128)].astype(F32).T.astype(BF16)

    loop(WIDTH // 128, turn)
    hub_spread.finish_cores()

    def assemble(table, first, parts, pieces):
        def body(t):
            at = {"x": t // 8, "y": lax.rem(t, 4)}
            core = lax.rem(t // 4, 2)
            blocks = []
            for z in range(4):
                at["z"] = z
                found = [p[(core,) + tuple(at[d] for d in order)] for p, (_, _, _, order) in zip(parts, pieces)]
                blocks.append(jnp.concatenate([f.astype(F32) for f in found], 1))
            table[pl.ds(pl.multiple_of(first + t * 32, 32), 32)] = jnp.concatenate(blocks, 0).astype(BF16)

        loop(32, body)

    assemble(hub_table, 0, hub_parts, HUB_PIECES)
    loads[0].wait()

    def before(i):
        cols = rows(i, 256)
        pre_self[:, cols] = dot(features[...], w_self[:, cols]) + bias[:, cols]
        total[:, cols] = dot(counts[:, :LOCAL], features[:, cols]) + dot(
            counts[:, LOCAL + SLOTS :], hub_table[:, cols]
        )

    loop(4, before)
    loads[2].wait()
    forward.wait_recv()

    def with_slots(i):
        cols = rows(i, 256)
        total[:, cols] += dot(counts[:, LOCAL : LOCAL + SLOTS], arrived[:, cols])

    loop(4, with_slots)

    def mean(i):
        scale = jnp.concatenate([inv_deg[rows(i, 64)]] * (WIDTH // 128), 1)
        aggregate[rows(i, 64)] = (total[rows(i, 64)] * scale).astype(BF16)

    loop(LOCAL // 64, mean)

    def act(i):
        m = rows(i, 128)
        pre = pre_self[m] + dot(aggregate[m], w_neigh[...])
        sigmoid = jax.nn.sigmoid(pre)
        hidden[m] = (pre * sigmoid).astype(BF16)
        slope = sigmoid * (1.0 + pre * (1.0 - sigmoid))
        d_pre[m] = (cotangent[m].astype(F32) * slope).astype(BF16)

    loop(LOCAL // 128, act)
    put_hidden = pltpu.make_async_copy(hidden, hidden_hbm, out_sem.at[0])
    put_hidden.start()

    def d_mean(i):
        cols = rows(i, 256)
        scale = jnp.concatenate([inv_deg[...]] * 2, 1)
        d_agg[:, cols] = (dot(d_pre[...], w_neigh_t[:, cols]) * scale).astype(BF16)

    loop(WIDTH // 256, d_mean)
    forward.wait_send()

    def d_slots(i):
        m = rows(i, 512)
        outgoing[m] = dot(counts_t[pl.ds(pl.multiple_of(LOCAL + i * 512, 512), 512)], d_agg[...]).astype(BF16)

    loop(SLOTS // 512, d_slots)
    backward.send(28)

    def keep_own(source, x, block):
        for core in range(2):
            if source == 0:
                own[0][core, x] = block[core].astype(BF16)
            elif source == 1:
                own[1][core, :, :, x] = block[core].astype(BF16)
            else:
                for y in range(4):
                    own[2][core, :, x, y] = block[core, y].astype(BF16)

    def grads_to(source, left):
        def body(i):
            block = dot(left[:, rows(i, 256)], d_pre[...], 0, 0).reshape(2, 4, 4, HUB, WIDTH)
            keep_own(source, i, block)

        loop(4, body)

    def d_hubs(i):
        base = LOCAL + SLOTS + i * 256
        block = dot(counts_t[pl.ds(pl.multiple_of(base, 256), 256)], d_agg[...])
        keep_own(2, i, block.reshape(2, 4, 4, HUB, WIDTH))

    def final_block(source, value):
        if source == 2:
            hub_back[...] = value
            return
        for part, (its_source, start, size, order) in zip(all_parts, GRAD_PIECES):
            if its_source == source:
                spot = (place["core"],) + tuple(place[d] for d in order)
                part[spot] = value[:, start : start + size].astype(BF16)

    reduce = Reduce(place, own, got, held, half, near, came, final_block, red_send, red_recv)
    spread = Spread(place, all_parts, [p[3] for p in GRAD_PIECES], [came[0]] * 4, all_send, all_recv)
    grads_to(0, features)
    first = reduce.start_core(0)
    grads_to(1, aggregate)
    second = reduce.start_core(1)
    backward.send(10)
    loop(4, d_hubs)
    third = reduce.start_core(2)
    reduce.finish_core(0, first)
    reduce.finish_core(1, second)
    reduce.finish_core(2, third)
    reduce.start_halves()
    backward.send(16)

    def own_grad(i):
        cols = rows(i, 256)
        total[:, cols] = dot(d_pre[...], w_self[cols], 1, 1) + dot(counts_t[:LOCAL], d_agg[:, cols])

    loop(4, own_grad)
    reduce.finish_halves()
    reduce.start_near()
    backward.send(20)
    reduce.finish_near()
    reduce.start_plane()
    backward.send(20)
    reduce.finish_plane()
    spread.start_plane()
    backward.send(18)
    spread.finish_plane()
    spread.start_last()
    backward.send(10)
    spread.relay()
    backward.send()
    backward.wait_recv()

    def final(i):
        cols = rows(i, 256)
        value = total[:, cols] + dot(picks_t[...], returned[:, cols])
        high = hub_back[:, cols].astype(BF16)
        low = (hub_back[:, cols] - high.astype(F32)).astype(BF16)
        both = jnp.concatenate([high.astype(F32), low.astype(F32)], 0).astype(BF16)
        grad_x[:, cols] = (value + dot(hub_picks[...], both, 0, 0)).astype(BF16)

    loop(4, final)
    put_grad_x = pltpu.make_async_copy(grad_x, grad_x_hbm, out_sem.at[1])
    put_grad_x.start()
    spread.finish_last()
    spread.finish_cores()
    puts = []
    for source, natural in enumerate((all_self, all_neigh)):
        pieces = [p for p in GRAD_PIECES if p[0] == source]
        parts = [part for part, p in zip(all_parts, GRAD_PIECES) if p[0] == source]
        assemble(arrived, source * WIDTH, parts, pieces)
        for k in range(4):
            put = pltpu.make_async_copy(
                arrived.at[pl.ds(source * WIDTH + k * 256, 256)],
                natural.at[pl.ds(k * 256, 256)],
                out_sem.at[2 + source * 4 + k],
            )
            put.start()
            puts.append(put)
    backward.wait_send()
    put_hidden.wait()
    put_grad_x.wait()
    for put in puts:
        put.wait()


def hand_out(*refs):
    sources, refs = refs[:4], refs[4:]
    results, bufs, (in_sem, out_sem) = refs[:4], refs[4:8], refs[8:]
    pieces = []
    for i, (src, dst, buf) in enumerate(zip(sources, results, bufs)):
        size = 256
        for k in range(src.shape[0] // size):
            part = pl.ds(k * size, size)
            slot = len(pieces)
            pieces.append(
                (
                    pltpu.make_async_copy(src.at[part], buf.at[part], in_sem.at[slot]),
                    pltpu.make_async_copy(buf.at[part], dst.at[part], out_sem.at[slot]),
                )
            )
    for load, _ in pieces:
        load.start()
    for load, store in pieces:
        load.wait()
        store.start()
    for _, store in pieces:
        store.wait()


def on_device(
    features, neighbours, degrees, send_rows, send_count, hub_rows, w_self, w_neigh, bias_term, cotangent
):
    vmem = pl.BlockSpec(memory_space=pltpu.VMEM)
    hbm = pl.BlockSpec(memory_space=pl.ANY)
    wide = (WIDTH,)

    def buf(*shape, kind=BF16):
        return pltpu.VMEM(shape, kind)

    part_bufs = [buf(2, 4, 4, 4, HUB, p[2]) for p in HUB_PIECES + GRAD_PIECES]
    for lead in ((2, 4, 4, 4), (4, 4, 4), (4, 4, 4), (4, 4), (2, 2, 4), (2, 4, 4), (15,)):
        part_bufs += [buf(*lead, HUB, WIDTH)] * 3
    dma = pltpu.SemaphoreType.DMA
    hidden, grad_x, grad_self, grad_neigh = pl.pallas_call(
        sage_kernel,
        out_shape=(
            jax.ShapeDtypeStruct((LOCAL, WIDTH), BF16),
            jax.ShapeDtypeStruct((LOCAL, WIDTH), BF16),
            jax.ShapeDtypeStruct((WIDTH, WIDTH), BF16),
            jax.ShapeDtypeStruct((WIDTH, WIDTH), BF16),
        ),
        in_specs=[vmem] * 5 + [pl.BlockSpec(memory_space=pltpu.SMEM)] + [vmem] + [hbm] * 3,
        out_specs=[hbm] * 4,
        scratch_shapes=[
            buf(LOCAL, WIDTH),
            buf(LOCAL, WIDTH),
            buf(WIDTH, WIDTH),
            buf(WIDTH, WIDTH),
            buf(WIDTH, WIDTH),
            buf(LOCAL, WIDTH),
            buf(LOCAL, SLOTS),
            buf(SLOT, LOCAL),
            buf(SLOTS, WIDTH),
            buf(SLOTS, WIDTH),
            buf(SLOTS, WIDTH),
            buf(HUBS, WIDTH),
            buf(FANOUT, 8, LOCAL, kind=jnp.int32),
            buf(TABLE, LOCAL),
            buf(LOCAL, TABLE),
            buf(LOCAL, 128, kind=F32),
            buf(LOCAL, WIDTH, kind=F32),
            buf(LOCAL, WIDTH, kind=F32),
            buf(LOCAL, WIDTH),
            buf(LOCAL, WIDTH),
            buf(LOCAL, WIDTH),
            buf(HUB, WIDTH, kind=F32),
            *part_bufs,
            dma((3,)),
            dma((10,)),
            dma,
            dma,
            dma,
            dma,
            dma((30,)),
            dma((30,)),
            dma((18,)),
            dma((18,)),
            dma((40,)),
            dma((40,)),
        ],
        compiler_params=pltpu.CompilerParams(
            collective_id=0, has_side_effects=True, vmem_limit_bytes=67043328
        ),
        name="sage",
    )(
        features,
        neighbours.T,
        degrees[None, :],
        send_rows,
        send_count,
        hub_rows,
        bias_term[None, :],
        w_self,
        w_neigh,
        cotangent,
    )
    results = (hidden, grad_x, grad_self, grad_neigh)
    return pl.pallas_call(
        hand_out,
        out_shape=tuple(jax.ShapeDtypeStruct(r.shape, r.dtype) for r in results),
        in_specs=[hbm] * 4,
        out_specs=[hbm] * 4,
        scratch_shapes=[buf(*r.shape) for r in results] + [dma((12,)), dma((12,))],
        name="hand_out",
    )(*results)


def solution(mesh):
    split = P(("row", "col"), None)
    in_specs = (split, split, P(("row", "col")), split, split, P(("row", "col")), P(), P(), P(), split)
    out_specs = (split, split, P(), P())
    return jax.shard_map(on_device, mesh=mesh, in_specs=in_specs, out_specs=out_specs, check_vma=False)
```

```python
import functools

import jax
import jax.numpy as jnp
from jax import lax
from jax.experimental import pallas as pl
from jax.experimental.pallas import tpu as pltpu
from jax.sharding import PartitionSpec as P

MESH = pl.DeviceIdType.MESH
F32 = jnp.float32
BF16 = jnp.bfloat16
WIDTH = 1024
LOCAL = 512
FANOUT = 16
SLOT = 16
HUB = 8
PEERS = 128
SLOTS = SLOT * PEERS
HUBS = HUB * PEERS
TABLE = LOCAL + SLOTS + HUBS
XYZ, YZX, ZXY = ("x", "y", "z"), ("y", "z", "x"), ("z", "x", "y")
HUB_PIECES = ((0, 0, 384, XYZ), (0, 384, 384, YZX), (0, 768, 256, ZXY))
GRAD_PIECES = ((0, 0, 640, XYZ), (1, 0, 640, YZX), (0, 640, 384, ZXY), (1, 640, 384, ZXY))
SUM_ORDERS = (XYZ, YZX, ZXY)


def where_am_i():
    row = lax.axis_index("row")
    col = lax.axis_index("col")
    return {"x": row // 2, "core": lax.rem(row, 2), "y": col // 4, "z": lax.rem(col, 4)}


def device_at(place):
    return (place["x"] * 2 + place["core"], place["y"] * 4 + place["z"])


def rank_of(place):
    return ((place["x"] * 2 + place["core"]) * 4 + place["y"]) * 4 + place["z"]


def shifted(place, dim, step):
    other = dict(place)
    other[dim] = lax.rem(place[dim] + step, 2 if dim == "core" else 4)
    return other


def message_order():
    left = [(x, c, y, z) for x in range(4) for y in range(4) for z in range(4) for c in range(2)][1:]
    load = [0] * 6
    order = []

    def after(offset):
        new = list(load)
        for axis, step in enumerate((offset[0], offset[2], offset[3])):
            if step in (1, 2):
                new[2 * axis] += 1
            if step in (2, 3):
                new[2 * axis + 1] += 1
        return new

    def unevenness(offset):
        new = after(offset)
        mean = sum(new) / 6
        return (max(new) - min(new), sum((v - mean) ** 2 for v in new), [(7 * v) % 4 for v in offset])

    while left:
        best = min(left, key=unevenness)
        left.remove(best)
        load[:] = after(best)
        order.append(best)
    return order


ORDER = message_order()
GROUP = 32


def opposite(offset):
    return ((4 - offset[0]) % 4, offset[1], (4 - offset[2]) % 4, (4 - offset[3]) % 4)


class Peers:
    def __init__(self, place):
        xs = [lax.rem(place["x"] + d, 4) for d in range(4)]
        cores = [place["core"], 1 - place["core"]]
        ys = [lax.rem(place["y"] + d, 4) for d in range(4)]
        zs = [lax.rem(place["z"] + d, 4) for d in range(4)]
        self.rows = [[x * 2 + c for c in cores] for x in xs]
        self.cols = [[y * 4 + z for z in zs] for y in ys]

    def device(self, offset):
        return (self.rows[offset[0]][offset[1]], self.cols[offset[2]][offset[3]])

    def rank(self, offset):
        row, col = self.device(offset)
        return row * 16 + col


def remote(src, dst, send_sem, recv_sem, peer):
    return pltpu.make_async_remote_copy(
        src_ref=src,
        dst_ref=dst,
        send_sem=send_sem,
        recv_sem=recv_sem,
        device_id=device_at(peer),
        device_id_type=MESH,
    )


def dot(a, b, ca=1, cb=0):
    return lax.dot_general(a, b, (((ca,), (cb,)), ((), ())), preferred_element_type=F32)


def loop(count, body):
    def step(i, carry):
        body(i)
        return carry

    lax.fori_loop(0, count, step, 0)


def rows(i, size):
    return pl.ds(pl.multiple_of(i * size, size), size)


PLANE = [(i, j) for i in range(4) for j in range(4)][1:]


def in_plane(place, order, steps):
    return shifted(shifted(place, order[1], steps[0]), order[2], steps[1])


def wait_for(ref, slot, send_sem, recv_sem):
    for sem in (send_sem, recv_sem):
        pltpu.make_async_copy(ref, ref, sem.at[slot]).wait()


class Exchange:
    def __init__(self, peers, me, src, dst, send_sem, recv_sem, back):
        self.peers, self.me, self.src, self.dst = peers, me, src, dst
        self.send_sem, self.recv_sem = send_sem, recv_sem
        self.back = back
        self.sent = 0

    def send(self, count=PEERS):
        for message in range(self.sent, min(self.sent + count, PEERS - 1)):
            here = pl.ds(message * SLOT, SLOT)
            if self.back:
                offset = opposite(ORDER[message])
                src, dst, recv_sem = self.src.at[here], self.dst.at[rows(self.me, SLOT)], self.recv_sem
            else:
                offset = ORDER[message]
                src, dst = self.src.at[rows(self.peers.rank(offset), SLOT)], self.dst.at[here]
                recv_sem = self.recv_sem.at[message // GROUP]
            pltpu.make_async_remote_copy(
                src_ref=src,
                dst_ref=dst,
                send_sem=self.send_sem,
                recv_sem=recv_sem,
                device_id=self.peers.device(offset),
                device_id_type=MESH,
            ).start()
        self.sent = min(self.sent + count, PEERS - 1)

    def wait_group(self, group):
        count = min(GROUP, PEERS - 1 - group * GROUP)
        part = pl.ds(group * GROUP * SLOT, count * SLOT)
        pltpu.make_async_copy(self.src.at[part], self.dst.at[part], self.recv_sem.at[group]).wait()

    def wait_recv(self):
        most = pl.ds(0, SLOTS - SLOT)
        pltpu.make_async_copy(self.src.at[most], self.dst.at[most], self.recv_sem).wait()

    def wait_send(self):
        most = pl.ds(0, SLOTS - SLOT)
        pltpu.make_async_copy(self.src.at[most], self.dst.at[most], self.send_sem).wait()


class Spread:
    def __init__(self, place, outs, orders, sizes, send_sem, recv_sem):
        self.place, self.outs, self.orders, self.sizes = place, outs, orders, sizes
        self.send_sem, self.recv_sem = send_sem, recv_sem

    def send(self, piece, spot, kind, peer):
        block = self.outs[piece].at[(self.place["core"],) + spot]
        slot = piece * 6 + kind
        copy = remote(block, block, self.send_sem.at[slot], self.recv_sem.at[slot], peer)
        copy.start()
        return copy

    def hand_over(self, piece, spot):
        self.send(piece, spot, 4, shifted(self.place, "core", 1))

    def start_plane(self):
        for steps in PLANE:
            for piece, order in enumerate(self.orders):
                spot = tuple(self.place[d] for d in order)
                self.send(piece, spot, 5, in_plane(self.place, order, steps))

    def finish_plane(self):
        for piece, size in enumerate(self.sizes):
            wait_for(size.at[:, :, : self.outs[piece].shape[-1]], piece * 6 + 5, self.send_sem, self.recv_sem)

    def start_last(self):
        self.copies = []
        for piece, order in enumerate(self.orders):
            spot = (self.place[order[0]],)
            up = self.send(piece, spot, 0, shifted(self.place, order[0], 1))
            down = self.send(piece, spot, 1, shifted(self.place, order[0], 3))
            self.copies.append((up, down))
        for piece, order in enumerate(self.orders):
            self.hand_over(piece, (self.place[order[0]],))

    def relay(self):
        relayed = []
        for piece, order in enumerate(self.orders):
            at, (up, down) = self.place[order[0]], self.copies[piece]
            below, above = lax.rem(at + 3, 4), lax.rem(at + 1, 4)
            up.wait()
            first = self.send(piece, (below, pl.ds(0, 2)), 2, shifted(self.place, order[0], 1))
            self.hand_over(piece, (below,))
            down.wait()
            second = self.send(piece, (above, pl.ds(2, 2)), 3, shifted(self.place, order[0], 3))
            self.hand_over(piece, (above,))
            relayed.append((first, second))
        self.copies = relayed

    def finish_last(self):
        for piece, order in enumerate(self.orders):
            far = lax.rem(self.place[order[0]] + 2, 4)
            for half, copy in enumerate(self.copies[piece]):
                copy.wait()
                self.hand_over(piece, (far, pl.ds(2 * half, 2)))

    def finish_cores(self):
        for piece, out in enumerate(self.outs):
            wait_for(out.at[0], piece * 6 + 4, self.send_sem, self.recv_sem)


class Reduce:
    def __init__(self, place, own, got, held, half, near, came, final, send_sem, recv_sem):
        self.place, self.own, self.got, self.held = place, own, got, held
        self.half, self.near, self.came, self.final = half, near, came, final
        self.send_sem, self.recv_sem = send_sem, recv_sem
        self.copies = []

    def send(self, src, dst, slot, peer):
        copy = remote(src, dst, self.send_sem.at[slot], self.recv_sem.at[slot], peer)
        copy.start()
        return copy

    def start_core(self, source):
        partner = shifted(self.place, "core", 1)
        return self.send(self.own[source].at[partner["core"]], self.got[source], source, partner)

    def finish_core(self, source, copy):
        core = self.place["core"]
        own, got, held = self.own[source], self.got[source], self.held[0][source]
        copy.wait()

        def add(t):
            a, b = t // 4, lax.rem(t, 4)
            held[a, b] = (own[core, a, b].astype(F32) + got[a, b].astype(F32)).astype(BF16)

        loop(16, add)

    def start_halves(self, source):
        order = SUM_ORDERS[source]
        far = lax.rem(self.place[order[0]] + 2, 4)
        for i, step in enumerate((1, 3)):
            part = self.held[0][source].at[far, pl.ds(2 * i, 2)]
            peer = shifted(self.place, order[0], step)
            self.copies.append(self.send(part, self.half[source].at[i], 3 + source * 2 + i, peer))

    def finish_halves(self):
        for source, order in enumerate(SUM_ORDERS):
            held, half = self.held[0][source], self.half[source]
            for i, step in enumerate((1, 3)):
                self.copies[source * 2 + i].wait()
                at = lax.rem(self.place[order[0]] + step, 4)
                for b in range(2):
                    value = held[at, 2 * i + b].astype(F32) + half[i, b].astype(F32)
                    held[at, 2 * i + b] = value.astype(BF16)

    def start_near(self):
        self.copies = []
        for source, order in enumerate(SUM_ORDERS):
            for i, step in enumerate((1, 3)):
                peer = shifted(self.place, order[0], step)
                part = self.held[0][source].at[peer[order[0]]]
                self.copies.append(self.send(part, self.near[source].at[i], 9 + source * 2 + i, peer))

    def finish_near(self):
        for source, order in enumerate(SUM_ORDERS):
            for i in range(2):
                self.copies[source * 2 + i].wait()
            held, near, at = self.held[0][source], self.near[source], self.place[order[0]]

            def fold(b, source=source, held=held, near=near, at=at):
                value = held[at, b].astype(F32) + near[0, b].astype(F32) + near[1, b].astype(F32)
                self.held[1][source][b] = value.astype(BF16)

            loop(4, fold)

    def start_plane(self):
        for k, steps in enumerate(PLANE):
            for source, order in enumerate(SUM_ORDERS):
                peer = in_plane(self.place, order, steps)
                part = self.held[1][source].at[peer[order[1]], peer[order[2]]]
                self.send(part, self.came[source].at[k], 15 + source, peer)

    def finish_plane(self):
        for source in range(3):
            wait_for(self.came[source], 15 + source, self.send_sem, self.recv_sem)
        for source, order in enumerate(SUM_ORDERS):
            value = self.held[1][source][self.place[order[1]], self.place[order[2]]].astype(F32)
            for k in range(15):
                value += self.came[source][k].astype(F32)
            self.final(source, value)


def sage_kernel(
    features,
    neighbours_t,
    degrees,
    send_rows,
    send_count,
    hub_rows,
    bias,
    w_self_hbm,
    w_neigh_hbm,
    cotangent_hbm,
    hidden_hbm,
    grad_x_hbm,
    all_self,
    all_neigh,
    hidden,
    grad_x,
    w_self,
    w_neigh,
    w_neigh_t,
    cotangent,
    picks_t,
    hub_picks,
    outgoing,
    arrived,
    returned,
    hub_table,
    nbr_wide,
    first_id,
    counts_t,
    counts,
    inv_deg,
    total,
    pre_self,
    aggregate,
    d_pre,
    d_agg,
    hub_back,
    *rest,
):
    groups, at = [], 0
    for size in (3, 4, 3, 3, 3, 3, 3, 3, 3):
        groups.append(rest[at : at + size])
        at += size
    hub_parts, all_parts, own, got, *held, half, near, came = groups
    (
        local_sem,
        out_sem,
        fwd_send,
        fwd_recv,
        bwd_send,
        bwd_recv,
        hub_send,
        hub_recv,
        red_send,
        red_recv,
        all_send,
        all_recv,
    ) = rest[28:]
    place = where_am_i()
    me = rank_of(place)
    barrier = pltpu.get_barrier_semaphore()

    peers = Peers(place)
    for offset in sorted(ORDER, key=lambda o: -sum(min(o[i], 4 - o[i]) for i in (0, 2, 3))):
        pl.semaphore_signal(barrier, inc=1, device_id=peers.device(offset), device_id_type=MESH)
    loads = [
        pltpu.make_async_copy(src, dst, local_sem.at[i])
        for i, (src, dst) in enumerate(((w_self_hbm, w_self), (w_neigh_hbm, w_neigh), (cotangent_hbm, cotangent)))
    ]
    for load in loads:
        load.start()

    owner = lax.broadcasted_iota(jnp.int32, (PEERS, SLOTS), 1) // SLOT
    widen = (owner == lax.broadcasted_iota(jnp.int32, (PEERS, SLOTS), 0)).astype(F32).astype(BF16)
    count = jnp.broadcast_to(send_count[...], (8, PEERS)).astype(F32).astype(BF16)
    count_wide = dot(count, widen)[0:1]
    place_in = lax.rem(lax.broadcasted_iota(jnp.int32, (1, SLOTS), 1), SLOT)
    live_row = jnp.where(place_in.astype(F32) < count_wide, send_rows[...], -1)

    def pick(i):
        row = lax.broadcasted_iota(jnp.int32, (64, SLOTS), 0) + i * 64
        picks_t[rows(i, 64)] = (row == live_row).astype(F32).astype(BF16)

    loop(LOCAL // 64, pick)

    def fill(i):
        outgoing[rows(i, 512)] = dot(picks_t[:, rows(i, 512)], features[...], 0, 0).astype(BF16)

    loop(SLOTS // 512, fill)
    which = lax.broadcasted_iota(jnp.int32, (SLOT, LOCAL), 0)
    chosen = jnp.zeros((SLOT, LOCAL), jnp.int32)
    for h in range(HUB):
        chosen = jnp.where(lax.rem(which, HUB) == h, hub_rows[h], chosen)
    hub_picks[...] = (chosen == lax.broadcasted_iota(jnp.int32, (SLOT, LOCAL), 1)).astype(F32).astype(BF16)
    own_hubs = dot(hub_picks[...], features[...])[:HUB]
    for part, (_, start, size, order) in zip(hub_parts, HUB_PIECES):
        part[(place["core"],) + tuple(place[d] for d in order)] = own_hubs[:, start : start + size].astype(BF16)
    arrived[SLOTS - SLOT :] = jnp.zeros((SLOT, WIDTH), BF16)
    returned[rows(me, SLOT)] = jnp.zeros((SLOT, WIDTH), BF16)

    forward = Exchange(peers, me, outgoing, arrived, fwd_send, fwd_recv, False)
    backward = Exchange(peers, me, outgoing, returned, bwd_send, bwd_recv, True)
    hub_spread = Spread(place, hub_parts, [p[3] for p in HUB_PIECES], [came[0]] * 3, hub_send, hub_recv)
    pl.semaphore_wait(barrier, PEERS - 1)

    live = lax.broadcasted_iota(jnp.int32, (FANOUT, LOCAL), 0) < degrees[...]
    target = jnp.where(live, neighbours_t[...], -1)
    for j in range(FANOUT):
        nbr_wide[j] = jnp.broadcast_to(target[j : j + 1], (8, LOCAL))
    inv_deg[...] = (1.0 / jnp.broadcast_to(degrees[...], (128, LOCAL)).astype(F32)).T

    def count_block(b):
        def strip(i):
            base = b * 128 + i * 32
            sums = [jnp.zeros((8, LOCAL), F32) for _ in range(4)]
            starts = [first_id[b * 8 + i * 2 + g // 2] + 8 * (g % 2) for g in range(4)]
            ids = [lax.broadcasted_iota(jnp.int32, (8, LOCAL), 0) + start for start in starts]
            for j in range(FANOUT):
                named = nbr_wide[j]
                for g in range(4):
                    sums[g] = sums[g] + jnp.where(named == ids[g], 1.0, 0.0)
            counts_t[pl.ds(pl.multiple_of(base, 32), 32)] = jnp.concatenate(sums, 0).astype(BF16)

        loop(4, strip)
        counts[:, rows(b, 128)] = counts_t[rows(b, 128)].astype(F32).T.astype(BF16)

    def count_blocks(low, high):
        loop(high - low, lambda i: count_block(low + i))

    hub_spread.start_plane()
    forward.send(30)

    def natural(e):
        first_id[e] = e * SLOT

    loop(LOCAL // SLOT, natural)
    loop(HUBS // SLOT, lambda e: natural((LOCAL + SLOTS) // SLOT + e))
    for message, offset in enumerate(ORDER):
        first_id[LOCAL // SLOT + message] = LOCAL + peers.rank(opposite(offset)) * SLOT
    first_id[LOCAL // SLOT + PEERS - 1] = -2 * SLOT
    count_blocks(0, 14)
    hub_spread.finish_plane()
    hub_spread.start_last()
    forward.send(40)
    count_blocks(14, 21)
    hub_spread.relay()
    forward.send()
    count_blocks(21, 28)
    hub_spread.finish_last()

    loads[1].wait()

    def turn(i):
        w_neigh_t[:, rows(i, 128)] = w_neigh[rows(i, 128)].astype(F32).T.astype(BF16)

    loop(WIDTH // 128, turn)
    hub_spread.finish_cores()

    def assemble(table, first, parts, pieces):
        def body(t):
            at = {"x": t // 8, "y": lax.rem(t, 4)}
            core = lax.rem(t // 4, 2)
            blocks = []
            for z in range(4):
                at["z"] = z
                found = [p[(core,) + tuple(at[d] for d in order)] for p, (_, _, _, order) in zip(parts, pieces)]
                blocks.append(jnp.concatenate([f.astype(F32) for f in found], 1))
            table[pl.ds(pl.multiple_of(first + t * 32, 32), 32)] = jnp.concatenate(blocks, 0).astype(BF16)

        loop(32, body)

    assemble(hub_table, 0, hub_parts, HUB_PIECES)
    loads[0].wait()

    def before(i):
        cols = rows(i, 256)
        pre_self[:, cols] = dot(features[...], w_self[:, cols]) + bias[:, cols]
        total[:, cols] = dot(counts[:, :LOCAL], features[:, cols]) + dot(
            counts[:, LOCAL + SLOTS :], hub_table[:, cols]
        )

    loop(4, before)
    loads[2].wait()

    def with_slots(group):
        span = group * GROUP * SLOT
        forward.wait_group(group)

        def body(i):
            cols = rows(i, 256)
            total[:, cols] += dot(
                counts[:, LOCAL + span : LOCAL + span + GROUP * SLOT], arrived[span : span + GROUP * SLOT, cols]
            )

        loop(4, body)

    for group in range(4):
        with_slots(group)

    def mean(i):
        scale = jnp.concatenate([inv_deg[rows(i, 64)]] * (WIDTH // 128), 1)
        aggregate[rows(i, 64)] = (total[rows(i, 64)] * scale).astype(BF16)

    loop(LOCAL // 64, mean)

    def act(i):
        m = rows(i, 128)
        pre = pre_self[m] + dot(aggregate[m], w_neigh[...])
        sigmoid = jax.nn.sigmoid(pre)
        hidden[m] = (pre * sigmoid).astype(BF16)
        slope = sigmoid * (1.0 + pre * (1.0 - sigmoid))
        d_pre[m] = (cotangent[m].astype(F32) * slope).astype(BF16)

    loop(LOCAL // 128, act)
    put_hidden = pltpu.make_async_copy(hidden, hidden_hbm, out_sem.at[0])
    put_hidden.start()

    def d_mean(i):
        cols = rows(i, 256)
        scale = jnp.concatenate([inv_deg[...]] * 2, 1)
        d_agg[:, cols] = (dot(d_pre[...], w_neigh_t[:, cols]) * scale).astype(BF16)

    loop(WIDTH // 256, d_mean)
    forward.wait_send()

    for i, messages in enumerate((8, 8, 8, 4)):
        block = dot(counts_t[LOCAL + i * 512 : LOCAL + (i + 1) * 512], d_agg[...])
        outgoing[i * 512 : (i + 1) * 512] = block.astype(BF16)
        backward.send(messages)

    def keep_own(source, x, block):
        for core in range(2):
            if source == 0:
                own[0][core, x] = block[core].astype(BF16)
            elif source == 1:
                own[1][core, :, :, x] = block[core].astype(BF16)
            else:
                for y in range(4):
                    own[2][core, :, x, y] = block[core, y].astype(BF16)

    def grads_to(source, left):
        def body(i):
            block = dot(left[:, rows(i, 256)], d_pre[...], 0, 0).reshape(2, 4, 4, HUB, WIDTH)
            keep_own(source, i, block)

        loop(4, body)

    def d_hubs(i):
        base = LOCAL + SLOTS + i * 256
        block = dot(counts_t[pl.ds(pl.multiple_of(base, 256), 256)], d_agg[...])
        keep_own(2, i, block.reshape(2, 4, 4, HUB, WIDTH))

    def final_block(source, value):
        if source == 2:
            hub_back[...] = value
            return
        for part, (its_source, start, size, order) in zip(all_parts, GRAD_PIECES):
            if its_source == source:
                spot = (place["core"],) + tuple(place[d] for d in order)
                part[spot] = value[:, start : start + size].astype(BF16)

    reduce = Reduce(place, own, got, held, half, near, came, final_block, red_send, red_recv)
    spread = Spread(place, all_parts, [p[3] for p in GRAD_PIECES], [came[0]] * 4, all_send, all_recv)
    grads_to(0, features)
    first = reduce.start_core(0)
    grads_to(1, aggregate)
    second = reduce.start_core(1)
    backward.send(8)
    reduce.finish_core(0, first)
    reduce.start_halves(0)
    loop(4, d_hubs)
    third = reduce.start_core(2)
    reduce.finish_core(1, second)
    reduce.start_halves(1)
    reduce.finish_core(2, third)
    reduce.start_halves(2)
    backward.send(12)

    def own_grad(i):
        cols = rows(i, 256)
        total[:, cols] = dot(d_pre[...], w_self[cols], 1, 1) + dot(counts_t[:LOCAL], d_agg[:, cols])

    loop(4, own_grad)
    reduce.finish_halves()
    reduce.start_near()
    backward.send(14)
    reduce.finish_near()
    reduce.start_plane()
    backward.send(14)
    reduce.finish_plane()
    spread.start_plane()
    backward.send(18)
    spread.finish_plane()
    spread.start_last()
    backward.send(18)
    spread.relay()
    backward.send()
    backward.wait_recv()

    def final(i):
        cols = rows(i, 256)
        value = total[:, cols] + dot(picks_t[...], returned[:, cols])
        high = hub_back[:, cols].astype(BF16)
        low = (hub_back[:, cols] - high.astype(F32)).astype(BF16)
        both = jnp.concatenate([high.astype(F32), low.astype(F32)], 0).astype(BF16)
        grad_x[:, cols] = (value + dot(hub_picks[...], both, 0, 0)).astype(BF16)

    loop(4, final)
    put_grad_x = pltpu.make_async_copy(grad_x, grad_x_hbm, out_sem.at[1])
    put_grad_x.start()
    spread.finish_last()
    spread.finish_cores()
    puts = []
    for source, natural in enumerate((all_self, all_neigh)):
        pieces = [p for p in GRAD_PIECES if p[0] == source]
        parts = [part for part, p in zip(all_parts, GRAD_PIECES) if p[0] == source]
        assemble(arrived, source * WIDTH, parts, pieces)
        for k in range(4):
            put = pltpu.make_async_copy(
                arrived.at[pl.ds(source * WIDTH + k * 256, 256)],
                natural.at[pl.ds(k * 256, 256)],
                out_sem.at[2 + source * 4 + k],
            )
            put.start()
            puts.append(put)
    backward.wait_send()
    put_hidden.wait()
    put_grad_x.wait()
    for put in puts:
        put.wait()


def hand_out(*refs):
    sources, refs = refs[:4], refs[4:]
    results, bufs, (in_sem, out_sem) = refs[:4], refs[4:8], refs[8:]
    pieces = []
    for i, (src, dst, buf) in enumerate(zip(sources, results, bufs)):
        size = 256
        for k in range(src.shape[0] // size):
            part = pl.ds(k * size, size)
            slot = len(pieces)
            pieces.append(
                (
                    pltpu.make_async_copy(src.at[part], buf.at[part], in_sem.at[slot]),
                    pltpu.make_async_copy(buf.at[part], dst.at[part], out_sem.at[slot]),
                )
            )
    for load, _ in pieces:
        load.start()
    for load, store in pieces:
        load.wait()
        store.start()
    for _, store in pieces:
        store.wait()


def on_device(
    features, neighbours, degrees, send_rows, send_count, hub_rows, w_self, w_neigh, bias_term, cotangent
):
    vmem = pl.BlockSpec(memory_space=pltpu.VMEM)
    hbm = pl.BlockSpec(memory_space=pl.ANY)
    wide = (WIDTH,)

    def buf(*shape, kind=BF16):
        return pltpu.VMEM(shape, kind)

    part_bufs = [buf(2, 4, 4, 4, HUB, p[2]) for p in HUB_PIECES + GRAD_PIECES]
    for lead in ((2, 4, 4, 4), (4, 4, 4), (4, 4, 4), (4, 4), (2, 2, 4), (2, 4, 4), (15,)):
        part_bufs += [buf(*lead, HUB, WIDTH)] * 3
    dma = pltpu.SemaphoreType.DMA
    hidden, grad_x, grad_self, grad_neigh = pl.pallas_call(
        sage_kernel,
        out_shape=(
            jax.ShapeDtypeStruct((LOCAL, WIDTH), BF16),
            jax.ShapeDtypeStruct((LOCAL, WIDTH), BF16),
            jax.ShapeDtypeStruct((WIDTH, WIDTH), BF16),
            jax.ShapeDtypeStruct((WIDTH, WIDTH), BF16),
        ),
        in_specs=[vmem] * 5 + [pl.BlockSpec(memory_space=pltpu.SMEM)] + [vmem] + [hbm] * 3,
        out_specs=[hbm] * 4,
        scratch_shapes=[
            buf(LOCAL, WIDTH),
            buf(LOCAL, WIDTH),
            buf(WIDTH, WIDTH),
            buf(WIDTH, WIDTH),
            buf(WIDTH, WIDTH),
            buf(LOCAL, WIDTH),
            buf(LOCAL, SLOTS),
            buf(SLOT, LOCAL),
            buf(SLOTS, WIDTH),
            buf(SLOTS, WIDTH),
            buf(SLOTS, WIDTH),
            buf(HUBS, WIDTH),
            buf(FANOUT, 8, LOCAL, kind=jnp.int32),
            pltpu.SMEM((TABLE // SLOT,), jnp.int32),
            buf(TABLE, LOCAL),
            buf(LOCAL, TABLE),
            buf(LOCAL, 128, kind=F32),
            buf(LOCAL, WIDTH, kind=F32),
            buf(LOCAL, WIDTH, kind=F32),
            buf(LOCAL, WIDTH),
            buf(LOCAL, WIDTH),
            buf(LOCAL, WIDTH),
            buf(HUB, WIDTH, kind=F32),
            *part_bufs,
            dma((3,)),
            dma((10,)),
            dma,
            dma((4,)),
            dma,
            dma,
            dma((18,)),
            dma((18,)),
            dma((18,)),
            dma((18,)),
            dma((24,)),
            dma((24,)),
        ],
        compiler_params=pltpu.CompilerParams(
            collective_id=0, has_side_effects=True, vmem_limit_bytes=67043328
        ),
        name="sage",
    )(
        features,
        neighbours.T,
        degrees[None, :],
        send_rows,
        send_count,
        hub_rows,
        bias_term[None, :],
        w_self,
        w_neigh,
        cotangent,
    )
    results = (hidden, grad_x, grad_self, grad_neigh)
    return pl.pallas_call(
        hand_out,
        out_shape=tuple(jax.ShapeDtypeStruct(r.shape, r.dtype) for r in results),
        in_specs=[hbm] * 4,
        out_specs=[hbm] * 4,
        scratch_shapes=[buf(*r.shape) for r in results] + [dma((12,)), dma((12,))],
        name="hand_out",
    )(*results)


def solution(mesh):
    split = P(("row", "col"), None)
    in_specs = (split, split, P(("row", "col")), split, split, P(("row", "col")), P(), P(), P(), split)
    out_specs = (split, split, P(), P())
    return jax.shard_map(on_device, mesh=mesh, in_specs=in_specs, out_specs=out_specs, check_vma=False)
```

```python
import functools

import jax
import jax.numpy as jnp
from jax import lax
from jax.experimental import pallas as pl
from jax.experimental.pallas import tpu as pltpu
from jax.sharding import PartitionSpec as P

MESH = pl.DeviceIdType.MESH
F32 = jnp.float32
BF16 = jnp.bfloat16
WIDTH = 1024
LOCAL = 512
FANOUT = 16
SLOT = 16
HUB = 8
PEERS = 128
SLOTS = SLOT * PEERS
HUBS = HUB * PEERS
TABLE = LOCAL + SLOTS + HUBS
XYZ, YZX, ZXY = ("x", "y", "z"), ("y", "z", "x"), ("z", "x", "y")
HUB_PIECES = ((0, 0, 384, XYZ), (0, 384, 384, YZX), (0, 768, 256, ZXY))
GRAD_PIECES = ((0, 0, 640, XYZ), (1, 0, 640, YZX), (0, 640, 384, ZXY), (1, 640, 384, ZXY))
SUM_ORDERS = (XYZ, YZX, ZXY)


def where_am_i():
    row = lax.axis_index("row")
    col = lax.axis_index("col")
    return {"x": row // 2, "core": lax.rem(row, 2), "y": col // 4, "z": lax.rem(col, 4)}


def device_at(place):
    return (place["x"] * 2 + place["core"], place["y"] * 4 + place["z"])


def rank_of(place):
    return ((place["x"] * 2 + place["core"]) * 4 + place["y"]) * 4 + place["z"]


def shifted(place, dim, step):
    other = dict(place)
    other[dim] = lax.rem(place[dim] + step, 2 if dim == "core" else 4)
    return other


def message_order():
    left = [(x, c, y, z) for x in range(4) for y in range(4) for z in range(4) for c in range(2)][1:]
    load = [0] * 6
    order = []

    def after(offset):
        new = list(load)
        for axis, step in enumerate((offset[0], offset[2], offset[3])):
            if step in (1, 2):
                new[2 * axis] += 1
            if step in (2, 3):
                new[2 * axis + 1] += 1
        return new

    def unevenness(offset):
        new = after(offset)
        mean = sum(new) / 6
        return (max(new) - min(new), sum((v - mean) ** 2 for v in new), [(7 * v) % 4 for v in offset])

    while left:
        best = min(left, key=unevenness)
        left.remove(best)
        load[:] = after(best)
        order.append(best)
    return order


ORDER = message_order()
GROUP = 32


def opposite(offset):
    return ((4 - offset[0]) % 4, offset[1], (4 - offset[2]) % 4, (4 - offset[3]) % 4)


class Peers:
    def __init__(self, place):
        xs = [lax.rem(place["x"] + d, 4) for d in range(4)]
        cores = [place["core"], 1 - place["core"]]
        ys = [lax.rem(place["y"] + d, 4) for d in range(4)]
        zs = [lax.rem(place["z"] + d, 4) for d in range(4)]
        self.rows = [[x * 2 + c for c in cores] for x in xs]
        self.cols = [[y * 4 + z for z in zs] for y in ys]

    def device(self, offset):
        return (self.rows[offset[0]][offset[1]], self.cols[offset[2]][offset[3]])

    def rank(self, offset):
        row, col = self.device(offset)
        return row * 16 + col


def remote(src, dst, send_sem, recv_sem, peer):
    return pltpu.make_async_remote_copy(
        src_ref=src,
        dst_ref=dst,
        send_sem=send_sem,
        recv_sem=recv_sem,
        device_id=device_at(peer),
        device_id_type=MESH,
    )


def dot(a, b, ca=1, cb=0):
    return lax.dot_general(a, b, (((ca,), (cb,)), ((), ())), preferred_element_type=F32)


def loop(count, body):
    def step(i, carry):
        body(i)
        return carry

    lax.fori_loop(0, count, step, 0)


def rows(i, size):
    return pl.ds(pl.multiple_of(i * size, size), size)


PLANE = [(i, j) for i in range(4) for j in range(4)][1:]


def in_plane(place, order, steps):
    return shifted(shifted(place, order[1], steps[0]), order[2], steps[1])


def wait_for(ref, slot, send_sem, recv_sem):
    for sem in (send_sem, recv_sem):
        pltpu.make_async_copy(ref, ref, sem.at[slot]).wait()


class Exchange:
    def __init__(self, peers, me, src, dst, send_sem, recv_sem, back):
        self.peers, self.me, self.src, self.dst = peers, me, src, dst
        self.send_sem, self.recv_sem = send_sem, recv_sem
        self.back = back
        self.sent = 0

    def send(self, count=PEERS):
        for message in range(self.sent, min(self.sent + count, PEERS - 1)):
            here = pl.ds(message * SLOT, SLOT)
            if self.back:
                offset = opposite(ORDER[message])
                src, dst, recv_sem = self.src.at[here], self.dst.at[rows(self.me, SLOT)], self.recv_sem
            else:
                offset = ORDER[message]
                src, dst = self.src.at[rows(self.peers.rank(offset), SLOT)], self.dst.at[here]
                recv_sem = self.recv_sem.at[message // GROUP]
            pltpu.make_async_remote_copy(
                src_ref=src,
                dst_ref=dst,
                send_sem=self.send_sem,
                recv_sem=recv_sem,
                device_id=self.peers.device(offset),
                device_id_type=MESH,
            ).start()
        self.sent = min(self.sent + count, PEERS - 1)

    def wait_group(self, group):
        count = min(GROUP, PEERS - 1 - group * GROUP)
        part = pl.ds(group * GROUP * SLOT, count * SLOT)
        pltpu.make_async_copy(self.src.at[part], self.dst.at[part], self.recv_sem.at[group]).wait()

    def wait_recv(self):
        most = pl.ds(0, SLOTS - SLOT)
        pltpu.make_async_copy(self.src.at[most], self.dst.at[most], self.recv_sem).wait()

    def wait_send(self):
        most = pl.ds(0, SLOTS - SLOT)
        pltpu.make_async_copy(self.src.at[most], self.dst.at[most], self.send_sem).wait()


class Spread:
    def __init__(self, place, outs, orders, sizes, send_sem, recv_sem):
        self.place, self.outs, self.orders, self.sizes = place, outs, orders, sizes
        self.send_sem, self.recv_sem = send_sem, recv_sem

    def send(self, piece, spot, kind, peer):
        block = self.outs[piece].at[(self.place["core"],) + spot]
        slot = piece * 6 + kind
        copy = remote(block, block, self.send_sem.at[slot], self.recv_sem.at[slot], peer)
        copy.start()
        return copy

    def hand_over(self, piece, spot):
        self.send(piece, spot, 4, shifted(self.place, "core", 1))

    def start_plane(self):
        for steps in PLANE:
            for piece, order in enumerate(self.orders):
                spot = tuple(self.place[d] for d in order)
                self.send(piece, spot, 5, in_plane(self.place, order, steps))

    def finish_plane(self):
        for piece, size in enumerate(self.sizes):
            wait_for(size.at[:, :, : self.outs[piece].shape[-1]], piece * 6 + 5, self.send_sem, self.recv_sem)

    def start_last(self):
        self.copies = []
        for piece, order in enumerate(self.orders):
            spot = (self.place[order[0]],)
            up = self.send(piece, spot, 0, shifted(self.place, order[0], 1))
            down = self.send(piece, spot, 1, shifted(self.place, order[0], 3))
            self.copies.append((up, down))
        for piece, order in enumerate(self.orders):
            self.hand_over(piece, (self.place[order[0]],))

    def relay(self):
        relayed = []
        for piece, order in enumerate(self.orders):
            at, (up, down) = self.place[order[0]], self.copies[piece]
            below, above = lax.rem(at + 3, 4), lax.rem(at + 1, 4)
            up.wait()
            first = self.send(piece, (below, pl.ds(0, 2)), 2, shifted(self.place, order[0], 1))
            self.hand_over(piece, (below,))
            down.wait()
            second = self.send(piece, (above, pl.ds(2, 2)), 3, shifted(self.place, order[0], 3))
            self.hand_over(piece, (above,))
            relayed.append((first, second))
        self.copies = relayed

    def finish_last(self):
        for piece, order in enumerate(self.orders):
            far = lax.rem(self.place[order[0]] + 2, 4)
            for half, copy in enumerate(self.copies[piece]):
                copy.wait()
                self.hand_over(piece, (far, pl.ds(2 * half, 2)))

    def finish_cores(self):
        for piece, out in enumerate(self.outs):
            wait_for(out.at[0], piece * 6 + 4, self.send_sem, self.recv_sem)


class Reduce:
    def __init__(self, place, own, got, held, half, near, came, final, send_sem, recv_sem):
        self.place, self.own, self.got, self.held = place, own, got, held
        self.half, self.near, self.came, self.final = half, near, came, final
        self.send_sem, self.recv_sem = send_sem, recv_sem
        self.copies = []

    def send(self, src, dst, slot, peer):
        copy = remote(src, dst, self.send_sem.at[slot], self.recv_sem.at[slot], peer)
        copy.start()
        return copy

    def start_core(self, source):
        partner = shifted(self.place, "core", 1)
        return self.send(self.own[source].at[partner["core"]], self.got[source], source, partner)

    def finish_core(self, source, copy):
        core = self.place["core"]
        own, got, held = self.own[source], self.got[source], self.held[0][source]
        copy.wait()

        def add(t):
            a, b = t // 4, lax.rem(t, 4)
            held[a, b] = (own[core, a, b].astype(F32) + got[a, b].astype(F32)).astype(BF16)

        loop(16, add)

    def start_halves(self, source):
        order = SUM_ORDERS[source]
        far = lax.rem(self.place[order[0]] + 2, 4)
        for i, step in enumerate((1, 3)):
            part = self.held[0][source].at[far, pl.ds(2 * i, 2)]
            peer = shifted(self.place, order[0], step)
            self.copies.append(self.send(part, self.half[source].at[i], 3 + source * 2 + i, peer))

    def finish_halves(self):
        for source, order in enumerate(SUM_ORDERS):
            held, half = self.held[0][source], self.half[source]
            for i, step in enumerate((1, 3)):
                self.copies[source * 2 + i].wait()
                at = lax.rem(self.place[order[0]] + step, 4)
                for b in range(2):
                    value = held[at, 2 * i + b].astype(F32) + half[i, b].astype(F32)
                    held[at, 2 * i + b] = value.astype(BF16)

    def start_near(self):
        self.copies = []
        for source, order in enumerate(SUM_ORDERS):
            for i, step in enumerate((1, 3)):
                peer = shifted(self.place, order[0], step)
                part = self.held[0][source].at[peer[order[0]]]
                self.copies.append(self.send(part, self.near[source].at[i], 9 + source * 2 + i, peer))

    def finish_near(self):
        for source, order in enumerate(SUM_ORDERS):
            for i in range(2):
                self.copies[source * 2 + i].wait()
            held, near, at = self.held[0][source], self.near[source], self.place[order[0]]

            def fold(b, source=source, held=held, near=near, at=at):
                value = held[at, b].astype(F32) + near[0, b].astype(F32) + near[1, b].astype(F32)
                self.held[1][source][b] = value.astype(BF16)

            loop(4, fold)

    def start_plane(self):
        for k, steps in enumerate(PLANE):
            for source, order in enumerate(SUM_ORDERS):
                peer = in_plane(self.place, order, steps)
                part = self.held[1][source].at[peer[order[1]], peer[order[2]]]
                self.send(part, self.came[source].at[k], 15 + source, peer)

    def finish_plane(self):
        for source in range(3):
            wait_for(self.came[source], 15 + source, self.send_sem, self.recv_sem)
        for source, order in enumerate(SUM_ORDERS):
            value = self.held[1][source][self.place[order[1]], self.place[order[2]]].astype(F32)
            for k in range(15):
                value += self.came[source][k].astype(F32)
            self.final(source, value)


def sage_kernel(
    features,
    neighbours_t,
    degrees,
    send_rows,
    send_count,
    hub_rows,
    bias,
    w_self_hbm,
    w_neigh_hbm,
    cotangent_hbm,
    hidden_hbm,
    grad_x_hbm,
    all_self,
    all_neigh,
    hidden,
    grad_x,
    w_self,
    w_neigh,
    w_neigh_t,
    cotangent,
    picks_t,
    hub_picks,
    outgoing,
    arrived,
    returned,
    hub_table,
    nbr_wide,
    first_id,
    counts_t,
    counts,
    inv_deg,
    total,
    pre_self,
    aggregate,
    d_pre,
    d_agg,
    hub_back,
    *rest,
):
    groups, at = [], 0
    for size in (3, 4, 3, 3, 3, 3, 3, 3, 3):
        groups.append(rest[at : at + size])
        at += size
    hub_parts, all_parts, own, got, *held, half, near, came = groups
    (
        local_sem,
        out_sem,
        fwd_send,
        fwd_recv,
        bwd_send,
        bwd_recv,
        hub_send,
        hub_recv,
        red_send,
        red_recv,
        all_send,
        all_recv,
    ) = rest[28:]
    place = where_am_i()
    me = rank_of(place)
    barrier = pltpu.get_barrier_semaphore()

    peers = Peers(place)
    for offset in sorted(ORDER, key=lambda o: -sum(min(o[i], 4 - o[i]) for i in (0, 2, 3))):
        pl.semaphore_signal(barrier, inc=1, device_id=peers.device(offset), device_id_type=MESH)
    loads = [
        pltpu.make_async_copy(src, dst, local_sem.at[i])
        for i, (src, dst) in enumerate(((w_self_hbm, w_self), (w_neigh_hbm, w_neigh), (cotangent_hbm, cotangent)))
    ]
    for load in loads:
        load.start()

    owner = lax.broadcasted_iota(jnp.int32, (PEERS, SLOTS), 1) // SLOT
    widen = (owner == lax.broadcasted_iota(jnp.int32, (PEERS, SLOTS), 0)).astype(F32).astype(BF16)
    count = jnp.broadcast_to(send_count[...], (8, PEERS)).astype(F32).astype(BF16)
    count_wide = dot(count, widen)[0:1]
    place_in = lax.rem(lax.broadcasted_iota(jnp.int32, (1, SLOTS), 1), SLOT)
    live_row = jnp.where(place_in.astype(F32) < count_wide, send_rows[...], -1)

    def pick(i):
        row = lax.broadcasted_iota(jnp.int32, (64, SLOTS), 0) + i * 64
        picks_t[rows(i, 64)] = (row == live_row).astype(F32).astype(BF16)

    loop(LOCAL // 64, pick)

    def fill(i):
        outgoing[rows(i, 512)] = dot(picks_t[:, rows(i, 512)], features[...], 0, 0).astype(BF16)

    loop(SLOTS // 512, fill)
    which = lax.broadcasted_iota(jnp.int32, (SLOT, LOCAL), 0)
    chosen = jnp.zeros((SLOT, LOCAL), jnp.int32)
    for h in range(HUB):
        chosen = jnp.where(lax.rem(which, HUB) == h, hub_rows[h], chosen)
    hub_picks[...] = (chosen == lax.broadcasted_iota(jnp.int32, (SLOT, LOCAL), 1)).astype(F32).astype(BF16)
    own_hubs = dot(hub_picks[...], features[...])[:HUB]
    for part, (_, start, size, order) in zip(hub_parts, HUB_PIECES):
        part[(place["core"],) + tuple(place[d] for d in order)] = own_hubs[:, start : start + size].astype(BF16)
    arrived[SLOTS - SLOT :] = jnp.zeros((SLOT, WIDTH), BF16)
    returned[rows(me, SLOT)] = jnp.zeros((SLOT, WIDTH), BF16)

    forward = Exchange(peers, me, outgoing, arrived, fwd_send, fwd_recv, False)
    backward = Exchange(peers, me, outgoing, returned, bwd_send, bwd_recv, True)
    hub_spread = Spread(place, hub_parts, [p[3] for p in HUB_PIECES], [came[0]] * 3, hub_send, hub_recv)
    pl.semaphore_wait(barrier, PEERS - 1)

    live = lax.broadcasted_iota(jnp.int32, (FANOUT, LOCAL), 0) < degrees[...]
    target = jnp.where(live, neighbours_t[...], -1)
    for j in range(FANOUT):
        nbr_wide[j] = jnp.broadcast_to(target[j : j + 1], (8, LOCAL))
    inv_deg[...] = (1.0 / jnp.broadcast_to(degrees[...], (128, LOCAL)).astype(F32)).T

    def count_block(b):
        def strip(i):
            base = b * 128 + i * 32
            sums = [jnp.zeros((8, LOCAL), F32) for _ in range(4)]
            starts = [first_id[b * 8 + i * 2 + g // 2] + 8 * (g % 2) for g in range(4)]
            ids = [lax.broadcasted_iota(jnp.int32, (8, LOCAL), 0) + start for start in starts]
            for j in range(FANOUT):
                named = nbr_wide[j]
                for g in range(4):
                    sums[g] = sums[g] + jnp.where(named == ids[g], 1.0, 0.0)
            counts_t[pl.ds(pl.multiple_of(base, 32), 32)] = jnp.concatenate(sums, 0).astype(BF16)

        loop(4, strip)
        counts[:, rows(b, 128)] = counts_t[rows(b, 128)].astype(F32).T.astype(BF16)

    def count_blocks(low, high):
        loop(high - low, lambda i: count_block(low + i))

    hub_spread.start_plane()
    forward.send(30)

    def natural(e):
        first_id[e] = e * SLOT

    loop(LOCAL // SLOT, natural)
    loop(HUBS // SLOT, lambda e: natural((LOCAL + SLOTS) // SLOT + e))
    for message, offset in enumerate(ORDER):
        first_id[LOCAL // SLOT + message] = LOCAL + peers.rank(opposite(offset)) * SLOT
    first_id[LOCAL // SLOT + PEERS - 1] = -2 * SLOT
    count_blocks(0, 14)
    hub_spread.finish_plane()
    hub_spread.start_last()
    forward.send(40)
    count_blocks(14, 21)
    hub_spread.relay()
    forward.send()
    count_blocks(21, 28)
    hub_spread.finish_last()

    loads[1].wait()

    def turn(i):
        w_neigh_t[:, rows(i, 128)] = w_neigh[rows(i, 128)].astype(F32).T.astype(BF16)

    loop(WIDTH // 128, turn)
    hub_spread.finish_cores()

    def assemble(table, first, parts, pieces):
        def body(t):
            at = {"x": t // 8, "y": lax.rem(t, 4)}
            core = lax.rem(t // 4, 2)
            blocks = []
            for z in range(4):
                at["z"] = z
                found = [p[(core,) + tuple(at[d] for d in order)] for p, (_, _, _, order) in zip(parts, pieces)]
                blocks.append(jnp.concatenate([f.astype(F32) for f in found], 1))
            table[pl.ds(pl.multiple_of(first + t * 32, 32), 32)] = jnp.concatenate(blocks, 0).astype(BF16)

        loop(32, body)

    assemble(hub_table, 0, hub_parts, HUB_PIECES)
    loads[0].wait()

    def before(i):
        cols = rows(i, 256)
        pre_self[:, cols] = dot(features[...], w_self[:, cols]) + bias[:, cols]
        total[:, cols] = dot(counts[:, :LOCAL], features[:, cols]) + dot(
            counts[:, LOCAL + SLOTS :], hub_table[:, cols]
        )

    loop(4, before)
    loads[2].wait()

    def with_slots(group):
        span = group * GROUP * SLOT
        forward.wait_group(group)

        def body(i):
            cols = rows(i, 256)
            total[:, cols] += dot(
                counts[:, LOCAL + span : LOCAL + span + GROUP * SLOT], arrived[span : span + GROUP * SLOT, cols]
            )

        loop(4, body)

    for group in range(4):
        with_slots(group)

    def mean(i):
        scale = jnp.concatenate([inv_deg[rows(i, 64)]] * (WIDTH // 128), 1)
        aggregate[rows(i, 64)] = (total[rows(i, 64)] * scale).astype(BF16)

    loop(LOCAL // 64, mean)

    def act(i):
        m = rows(i, 128)
        pre = pre_self[m] + dot(aggregate[m], w_neigh[...])
        sigmoid = jax.nn.sigmoid(pre)
        hidden[m] = (pre * sigmoid).astype(BF16)
        slope = sigmoid * (1.0 + pre * (1.0 - sigmoid))
        d_pre[m] = (cotangent[m].astype(F32) * slope).astype(BF16)

    loop(LOCAL // 128, act)
    put_hidden = pltpu.make_async_copy(hidden, hidden_hbm, out_sem.at[0])
    put_hidden.start()

    def d_mean(i):
        cols = rows(i, 256)
        scale = jnp.concatenate([inv_deg[...]] * 2, 1)
        d_agg[:, cols] = (dot(d_pre[...], w_neigh_t[:, cols]) * scale).astype(BF16)

    loop(WIDTH // 256, d_mean)
    forward.wait_send()

    for i, messages in enumerate((8, 8, 8, 4)):
        block = dot(counts_t[LOCAL + i * 512 : LOCAL + (i + 1) * 512], d_agg[...])
        outgoing[i * 512 : (i + 1) * 512] = block.astype(BF16)
        backward.send(messages)

    def keep_own(source, x, block):
        for core in range(2):
            if source == 0:
                own[0][core, x] = block[core].astype(BF16)
            elif source == 1:
                own[1][core, :, :, x] = block[core].astype(BF16)
            else:
                for y in range(4):
                    own[2][core, :, x, y] = block[core, y].astype(BF16)

    def grads_to(source, left):
        def body(i):
            block = dot(left[:, rows(i, 256)], d_pre[...], 0, 0).reshape(2, 4, 4, HUB, WIDTH)
            keep_own(source, i, block)

        loop(4, body)

    def d_hubs(i):
        base = LOCAL + SLOTS + i * 256
        block = dot(counts_t[pl.ds(pl.multiple_of(base, 256), 256)], d_agg[...])
        keep_own(2, i, block.reshape(2, 4, 4, HUB, WIDTH))

    def final_block(source, value):
        if source == 2:
            hub_back[...] = value
            return
        for part, (its_source, start, size, order) in zip(all_parts, GRAD_PIECES):
            if its_source == source:
                spot = (place["core"],) + tuple(place[d] for d in order)
                part[spot] = value[:, start : start + size].astype(BF16)

    reduce = Reduce(place, own, got, held, half, near, came, final_block, red_send, red_recv)
    spread = Spread(place, all_parts, [p[3] for p in GRAD_PIECES], [came[0]] * 4, all_send, all_recv)
    grads_to(0, features)
    first = reduce.start_core(0)
    grads_to(1, aggregate)
    second = reduce.start_core(1)
    backward.send(8)
    reduce.finish_core(0, first)
    reduce.start_halves(0)
    loop(4, d_hubs)
    third = reduce.start_core(2)
    reduce.finish_core(1, second)
    reduce.start_halves(1)
    reduce.finish_core(2, third)
    reduce.start_halves(2)
    backward.send(12)

    def own_grad(i):
        cols = rows(i, 256)
        total[:, cols] = dot(d_pre[...], w_self[cols], 1, 1) + dot(counts_t[:LOCAL], d_agg[:, cols])

    loop(4, own_grad)
    reduce.finish_halves()
    reduce.start_near()
    backward.send(14)
    reduce.finish_near()
    reduce.start_plane()
    backward.send(14)
    reduce.finish_plane()
    spread.start_plane()
    backward.send(18)
    spread.finish_plane()
    spread.start_last()
    backward.send(22)
    spread.relay()
    backward.send()
    backward.wait_recv()

    def final(i):
        cols = rows(i, 256)
        value = total[:, cols] + dot(picks_t[...], returned[:, cols])
        high = hub_back[:, cols].astype(BF16)
        low = (hub_back[:, cols] - high.astype(F32)).astype(BF16)
        both = jnp.concatenate([high.astype(F32), low.astype(F32)], 0).astype(BF16)
        grad_x[:, cols] = (value + dot(hub_picks[...], both, 0, 0)).astype(BF16)

    loop(4, final)
    put_grad_x = pltpu.make_async_copy(grad_x, grad_x_hbm, out_sem.at[1])
    put_grad_x.start()
    spread.finish_last()
    spread.finish_cores()
    puts = []
    for source, natural in enumerate((all_self, all_neigh)):
        pieces = [p for p in GRAD_PIECES if p[0] == source]
        parts = [part for part, p in zip(all_parts, GRAD_PIECES) if p[0] == source]
        assemble(arrived, source * WIDTH, parts, pieces)
        for k in range(4):
            put = pltpu.make_async_copy(
                arrived.at[pl.ds(source * WIDTH + k * 256, 256)],
                natural.at[pl.ds(k * 256, 256)],
                out_sem.at[2 + source * 4 + k],
            )
            put.start()
            puts.append(put)
    backward.wait_send()
    put_hidden.wait()
    put_grad_x.wait()
    for put in puts:
        put.wait()


def hand_out(*refs):
    sources, refs = refs[:4], refs[4:]
    results, bufs, (in_sem, out_sem) = refs[:4], refs[4:8], refs[8:]
    pieces = []
    for i, (src, dst, buf) in enumerate(zip(sources, results, bufs)):
        size = 256
        for k in range(src.shape[0] // size):
            part = pl.ds(k * size, size)
            slot = len(pieces)
            pieces.append(
                (
                    pltpu.make_async_copy(src.at[part], buf.at[part], in_sem.at[slot]),
                    pltpu.make_async_copy(buf.at[part], dst.at[part], out_sem.at[slot]),
                )
            )
    for load, _ in pieces:
        load.start()
    for load, store in pieces:
        load.wait()
        store.start()
    for _, store in pieces:
        store.wait()


def on_device(
    features, neighbours, degrees, send_rows, send_count, hub_rows, w_self, w_neigh, bias_term, cotangent
):
    vmem = pl.BlockSpec(memory_space=pltpu.VMEM)
    hbm = pl.BlockSpec(memory_space=pl.ANY)
    wide = (WIDTH,)

    def buf(*shape, kind=BF16):
        return pltpu.VMEM(shape, kind)

    part_bufs = [buf(2, 4, 4, 4, HUB, p[2]) for p in HUB_PIECES + GRAD_PIECES]
    for lead in ((2, 4, 4, 4), (4, 4, 4), (4, 4, 4), (4, 4), (2, 2, 4), (2, 4, 4), (15,)):
        part_bufs += [buf(*lead, HUB, WIDTH)] * 3
    dma = pltpu.SemaphoreType.DMA
    hidden, grad_x, grad_self, grad_neigh = pl.pallas_call(
        sage_kernel,
        out_shape=(
            jax.ShapeDtypeStruct((LOCAL, WIDTH), BF16),
            jax.ShapeDtypeStruct((LOCAL, WIDTH), BF16),
            jax.ShapeDtypeStruct((WIDTH, WIDTH), BF16),
            jax.ShapeDtypeStruct((WIDTH, WIDTH), BF16),
        ),
        in_specs=[vmem] * 5 + [pl.BlockSpec(memory_space=pltpu.SMEM)] + [vmem] + [hbm] * 3,
        out_specs=[hbm] * 4,
        scratch_shapes=[
            buf(LOCAL, WIDTH),
            buf(LOCAL, WIDTH),
            buf(WIDTH, WIDTH),
            buf(WIDTH, WIDTH),
            buf(WIDTH, WIDTH),
            buf(LOCAL, WIDTH),
            buf(LOCAL, SLOTS),
            buf(SLOT, LOCAL),
            buf(SLOTS, WIDTH),
            buf(SLOTS, WIDTH),
            buf(SLOTS, WIDTH),
            buf(HUBS, WIDTH),
            buf(FANOUT, 8, LOCAL, kind=jnp.int32),
            pltpu.SMEM((TABLE // SLOT,), jnp.int32),
            buf(TABLE, LOCAL),
            buf(LOCAL, TABLE),
            buf(LOCAL, 128, kind=F32),
            buf(LOCAL, WIDTH, kind=F32),
            buf(LOCAL, WIDTH, kind=F32),
            buf(LOCAL, WIDTH),
            buf(LOCAL, WIDTH),
            buf(LOCAL, WIDTH),
            buf(HUB, WIDTH, kind=F32),
            *part_bufs,
            dma((3,)),
            dma((10,)),
            dma,
            dma((4,)),
            dma,
            dma,
            dma((18,)),
            dma((18,)),
            dma((18,)),
            dma((18,)),
            dma((24,)),
            dma((24,)),
        ],
        compiler_params=pltpu.CompilerParams(
            collective_id=0, has_side_effects=True, vmem_limit_bytes=67043328
        ),
        name="sage",
    )(
        features,
        neighbours.T,
        degrees[None, :],
        send_rows,
        send_count,
        hub_rows,
        bias_term[None, :],
        w_self,
        w_neigh,
        cotangent,
    )
    results = (hidden, grad_x, grad_self, grad_neigh)
    return pl.pallas_call(
        hand_out,
        out_shape=tuple(jax.ShapeDtypeStruct(r.shape, r.dtype) for r in results),
        in_specs=[hbm] * 4,
        out_specs=[hbm] * 4,
        scratch_shapes=[buf(*r.shape) for r in results] + [dma((12,)), dma((12,))],
        name="hand_out",
    )(*results)


def solution(mesh):
    split = P(("row", "col"), None)
    in_specs = (split, split, P(("row", "col")), split, split, P(("row", "col")), P(), P(), P(), split)
    out_specs = (split, split, P(), P())
    return jax.shard_map(on_device, mesh=mesh, in_specs=in_specs, out_specs=out_specs, check_vma=False)
```
